256 devices in a mesh: rows: 64 (over x_hi, y, z), grp: 4 (over x_lo, core).
Axes of the slice: x: 4 (x_hi: 2, x_lo: 2; x = x_hi * 2 + x_lo), y: 4, z: 8, core: 2. Of those that a mesh axis runs over, the one named last changes fastest.
Arguments:
- table: float32 [524288, 256], P(('rows', 'grp')), may hold values from -1.5 to 1.5
- hot_slot: int32 [4096], P(('rows', 'grp')), may hold values from 0 to 2047, as said below
- cold_row: int32 [256, 256, 8], P(('rows', 'grp')), may hold values from 0 to 2047, as said below
- cold_bag: int32 [256, 256, 8], P(('rows', 'grp')), may hold values from 0 to 511
- hot_pick: int32 [65536, 8], P(('rows', 'grp')), may hold values from 0 to 4095
- dense: float32 [65536, 256], P(('rows', 'grp')), may hold values from -6 to 6
- label: int32 [65536], P(('rows', 'grp')), may hold values 0 or 1
Outputs:
- pooled: float32 [65536, 256], P(('rows', 'grp'))
- new_table: float32 [524288, 256], P(('rows', 'grp'))
- hot_new: float32 [4096, 256], replicated
The draws below stay inside these ranges and needn't reach their ends.
Inputs may be any that keep to these rules, and one draw needn't show every extreme that they name: `hot_slot`: distinct within each device's block of 16 entries; hot row h lies in the shard of device h // 16. `cold_row`: a cold slot never names a hot row of its owner. `cold_bag`: a value of 256 or more marks an empty slot.
All inputs are finite; a program needn't handle non-finite values. No bound on the sum of `label` on one device may be relied on, other than what follows from the above.
Results may differ from the reference program's by a relative error of at most 0.0029.
Values may be sent and summed in bfloat16 or wider, within the bound.
A program may use at most 64 MiB of HBM per device.

```python
import jax
import jax.numpy as jnp
from jax import lax

DIM = 256
ROWS_DEV = 2048
HOT_DEV = 16
B_DEV = 256
HBAG = 8
CAP = 8
TABLE_ROWS = 524288
HOT = 4096
BATCH = 65536
DEVICES = 256


def shard_orders(key):
    keys = jax.random.split(jax.random.fold_in(key, 7), DEVICES)
    return jax.vmap(lambda k: jax.random.permutation(k, ROWS_DEV))(keys).astype(jnp.int32)


def draw_hot_slot(key, part):
    orders = shard_orders(key)
    return orders[:, :HOT_DEV].reshape(HOT).astype(jnp.int32)


def draw_cold_row(key, part):
    orders = shard_orders(key)
    picks = jax.random.randint(jax.random.fold_in(key, 11), (DEVICES, DEVICES, CAP), 0, ROWS_DEV - HOT_DEV) + HOT_DEV

    def one_source(pick):
        return jnp.take_along_axis(orders, pick, axis=1)
    return jax.vmap(one_source)(picks).astype(jnp.int32)


def with_ends(values, own_key, low, high):
    extent = values.shape
    place = [jax.random.randint(jax.random.fold_in(own_key, axis), (), 0, extent[axis]) for axis in range(len(extent))]
    values = values.at[tuple(place)].set(low)
    longest = extent.index(max(extent))
    place[longest] = (place[longest] + 1) % extent[longest]
    return values.at[tuple(place)].set(high)


def steps_of(rng, dims, shards, least, top_value):
    def one(dim, blocks):
        heights = jax.random.uniform(jax.random.fold_in(jax.random.fold_in(rng, 6), dim), (blocks,), jnp.float32, least / len(shards), top_value / len(shards))
        return jnp.repeat(jnp.exp(heights), dims[dim] // blocks).reshape((-1,) + (1,) * (len(dims) - dim - 1))

    gain = one(*shards[0])
    for cut in shards[1:]:
        gain = gain * one(*cut)
    return gain


def noise(rng, shape, width, most, shards=(), kind=jnp.bfloat16):
    result = width * jax.random.normal(rng, shape, jnp.float32)
    if shards:
        result = result * steps_of(rng, shape, shards, -0.22, 0.18)
    return jnp.clip(result, -most, most).astype(kind)


def setup_inputs(seed: int = 0) -> dict:
    seeds = jax.random.split(jax.random.key(seed), 8)
    return {
        "table": noise(seeds[0], (TABLE_ROWS, DIM), 0.25, 1.5, ((0, 256),), jnp.float32),
        "hot_slot": draw_hot_slot(jax.random.fold_in(seeds[7], 71), 0),
        "cold_row": draw_cold_row(jax.random.fold_in(seeds[7], 71), 0),
        "cold_bag": with_ends(jax.random.randint(seeds[3], (DEVICES, DEVICES, CAP), 0, 2 * B_DEV), jax.random.fold_in(seeds[3], 1), 0, (2 * B_DEV) - 1).astype(jnp.int32),
        "hot_pick": with_ends(jax.random.randint(seeds[4], (BATCH, HBAG), 0, HOT), jax.random.fold_in(seeds[4], 1), 0, HOT - 1).astype(jnp.int32),
        "dense": noise(seeds[5], (BATCH, DIM), 1.0, 6.0, ((0, 256),), jnp.float32),
        "label": with_ends((jax.random.randint(seeds[6], (BATCH,), 0, 2) < 1).astype(jnp.int32), jax.random.fold_in(seeds[6], 1), 0, 1),
    }


def reference(table, hot_slot, cold_row, cold_bag, hot_pick, dense, label):
    rounded = table.astype(jnp.bfloat16)
    owners = jnp.arange(DEVICES, dtype=jnp.int32)
    cold_id = (owners * ROWS_DEV)[None, :, None] + cold_row
    hot_id = (jnp.arange(HOT, dtype=jnp.int32) // HOT_DEV) * ROWS_DEV + hot_slot
    samples = jnp.arange(B_DEV, dtype=jnp.int32)

    def pool_one(args):
        ids, bags = args
        emb = rounded[ids.reshape(-1)]
        onehot = (samples[:, None] == bags.reshape(-1)[None, :]).astype(jnp.bfloat16)
        return jnp.dot(onehot, emb, preferred_element_type=jnp.float32)

    cold_pooled = lax.map(pool_one, (cold_id, cold_bag)).reshape(BATCH, DIM)
    hot_rows = rounded[hot_id]
    hot_pooled = jnp.sum(hot_rows[hot_pick].astype(jnp.float32), axis=1)
    pooled = cold_pooled + hot_pooled
    score = jnp.sum(pooled * dense, axis=1) / (DIM ** 0.5)
    err = jax.nn.sigmoid(score) - label.astype(jnp.float32)
    grad = err[:, None] * dense
    live = cold_bag < B_DEV
    source = (jnp.arange(DEVICES, dtype=jnp.int32) * B_DEV)[:, None, None]
    index = source + jnp.minimum(cold_bag, B_DEV - 1)
    table_grad = jnp.zeros((TABLE_ROWS, DIM), jnp.float32)

    def add_source(acc, args):
        idx, alive, ids = args
        slot_grad = jnp.where(alive.reshape(-1)[:, None], grad[idx.reshape(-1)], 0.0)
        return acc.at[ids.reshape(-1)].add(slot_grad), None

    table_grad, _ = lax.scan(add_source, table_grad, (index, live, cold_id))
    picked = hot_id[hot_pick].reshape(-1)
    spread = jnp.repeat(grad, HBAG, axis=0)
    table_grad = table_grad.at[picked].add(spread)
    new_table = table - 0.1 * table_grad
    hot_new = new_table[hot_id]
    return pooled, new_table, hot_new
```

```python
import jax
import jax.numpy as jnp
from jax import lax
from jax.sharding import PartitionSpec as P

AXES = ("rows", "grp")


def exchange(blocks):
    return lax.all_to_all(blocks, AXES, split_axis=0, concat_axis=0, tiled=True)


def split_bf16(value):
    high = lax.reduce_precision(value, exponent_bits=8, mantissa_bits=7)
    return high.astype(jnp.bfloat16), (value - high).astype(jnp.bfloat16)


def body(table, hot_slot, cold_row, cold_bag, hot_pick, dense, label):
    n = lax.axis_size("rows") * lax.axis_size("grp")
    n_table, width = table.shape
    samples = dense.shape[0]
    own_hot = hot_slot.shape[0]
    cap = cold_row.shape[2]
    slots = cold_row.shape[1] * cap
    f32, bf16 = jnp.float32, jnp.bfloat16
    rounded = table.astype(bf16)

    arrived = exchange(cold_row[0]).reshape(slots)
    hot_old = table[hot_slot]
    hot_copy = exchange(jnp.broadcast_to(hot_old.astype(bf16)[None], (n, own_hot, width)))
    hot_copy = hot_copy.reshape(n * own_hot, width)

    row_ids = jnp.arange(n_table, dtype=jnp.int32)
    at_row = (arrived[:, None] == row_ids[None, :]).astype(bf16)
    looked = jnp.dot(at_row, rounded, preferred_element_type=f32).astype(bf16)
    returned = exchange(looked.reshape(n, cap, width)).reshape(slots, width)

    bags = cold_bag[0].reshape(slots)
    sample_ids = jnp.arange(samples, dtype=jnp.int32)
    selector = (sample_ids[:, None] == bags[None, :]).astype(bf16)
    hot_ids = jnp.arange(n * own_hot, dtype=jnp.int32)
    counts = sum(
        (hot_pick[:, j][:, None] == hot_ids[None, :]).astype(f32)
        for j in range(hot_pick.shape[1])
    ).astype(bf16)
    pooled = jnp.dot(selector, returned, preferred_element_type=f32)
    pooled = pooled + jnp.dot(counts, hot_copy, preferred_element_type=f32)
    score = jnp.sum(pooled * dense, axis=1) / width**0.5
    err = jax.nn.sigmoid(score) - label.astype(f32)
    grad = err[:, None] * dense
    high, low = split_bf16(grad)

    first = (((0,), (0,)), ((), ()))
    slot_grad = lax.dot_general(selector, high, first, preferred_element_type=f32).astype(bf16)
    delivered = exchange(slot_grad.reshape(n, cap, width)).reshape(slots, width)

    hot_local = lax.dot_general(counts, high, first, preferred_element_type=f32)
    hot_local = hot_local + lax.dot_general(counts, low, first, preferred_element_type=f32)
    parts = exchange(hot_local.astype(bf16).reshape(n, own_hot, width))
    own_grad = jnp.sum(parts.astype(f32), axis=0)
    hot_own_new = hot_old - 0.1 * own_grad
    hot_new = exchange(jnp.broadcast_to(hot_own_new.astype(bf16)[None], (n, own_hot, width)))
    hot_new = hot_new.reshape(n * own_hot, width).astype(f32)

    table_grad = lax.dot_general(at_row, delivered, first, preferred_element_type=f32)
    at_hot = (row_ids[:, None] == hot_slot[None, :]).astype(f32)
    table_grad = table_grad + jnp.dot(
        at_hot, own_grad, precision=lax.Precision.HIGHEST, preferred_element_type=f32
    )
    new_table = table - 0.1 * table_grad
    return (pooled, new_table, hot_new)


def solution(mesh):
    placed = (
        P(AXES, None),
        P(AXES),
        P(AXES, None, None),
        P(AXES, None, None),
        P(AXES, None),
        P(AXES, None),
        P(AXES),
    )
    return jax.shard_map(
        body,
        mesh=mesh,
        in_specs=placed,
        out_specs=(P(AXES, None), P(AXES, None), P()),
        check_vma=False,
    )
```

```python
import functools
import math

import jax
import jax.numpy as jnp
from jax import lax
from jax.experimental import pallas as pl
from jax.experimental.pallas import tpu as pltpu
from jax.sharding import PartitionSpec as P

AXES = ("rows", "grp")
MESH = pl.DeviceIdType.MESH
SHAPE = (2, 4, 8, 2, 2)


def exchange(blocks):
    return lax.all_to_all(blocks, AXES, split_axis=0, concat_axis=0, tiled=True)


def split_bf16(value):
    high = lax.reduce_precision(value, exponent_bits=8, mantissa_bits=7)
    return high.astype(jnp.bfloat16), (value - high).astype(jnp.bfloat16)


class Place:
    def __init__(self, dims):
        self.dims = dims
        x_hi, y, z, x_lo, core = dims
        r, g = lax.axis_index("rows"), lax.axis_index("grp")
        self.x_hi, self.y, self.z = r // (y * z), (r // z) % y, r % z
        self.x_lo, self.c = g // core, g % core
        self.x = self.x_hi * x_lo + self.x_lo
        self.n = (x_hi * x_lo, y, z)

    def device(self, x, y, z, c):
        _, n_y, n_z, n_lo, n_core = self.dims
        return ((x // n_lo * n_y + y) * n_z + z, x % n_lo * n_core + c)

    def along_x(self, k):
        x = (self.x + k) % self.n[0]
        return x, self.device(x, self.y, self.z, self.c)

    def along_y(self, k):
        y = (self.y + k) % self.n[1]
        return y, self.device(self.x, y, self.z, self.c)

    def along_z(self, k):
        z = (self.z + k) % self.n[2]
        return z, self.device(self.x, self.y, z, self.c)

    def partner(self):
        return self.device(self.x, self.y, self.z, 1 - self.c)

    def meet(self):
        barrier = pltpu.get_barrier_semaphore()
        n_x, n_y, n_z = self.n
        peers = [self.along_z(k)[1] for k in range(1, n_z)]
        peers += [self.along_y(k)[1] for k in range(1, n_y)]
        peers += [self.along_x(k)[1] for k in range(1, n_x)]
        peers += [self.partner()]
        for peer in peers:
            pl.semaphore_signal(barrier, inc=1, device_id=peer, device_id_type=MESH)
        pl.semaphore_wait(barrier, len(peers))


def copies_of_gather(dims):
    n_x, n_y, n_z = dims[0] * dims[3], dims[1], dims[2]
    return (n_z - 1) + 2 * (n_y - 1) + 2 * (n_x - 1) + 1


def copies_of_scatter(dims):
    return copies_of_gather(dims)


class Sender:
    def __init__(self, send_sem, recv_sem):
        self.send_sem, self.recv_sem = send_sem, recv_sem
        self.used = 0
        self.all = []

    def start(self, src, dst, device):
        copy = pltpu.make_async_remote_copy(
            src_ref=src,
            dst_ref=dst,
            send_sem=self.send_sem.at[self.used],
            recv_sem=self.recv_sem.at[self.used],
            device_id=device,
            device_id_type=MESH,
        )
        copy.start()
        self.used += 1
        self.all.append(copy)
        return copy

    def finish(self):
        for copy in self.all:
            copy.wait_send()


def gather_rows(me, own, full, sender, local_sem):
    n_x, n_y, n_z = me.n
    half = n_z // 2
    mine = full.at[me.x_hi, me.y, me.z, me.x_lo, me.c]
    keep = pltpu.make_async_copy(own, mine, local_sem)
    keep.start()
    stage = [sender.start(own, mine, me.along_z(k)[1]) for k in range(1, n_z)]
    keep.wait()
    for copy in stage:
        copy.wait_recv()
    low, top = pl.ds(0, half), pl.ds(half, half)
    line = full.at[me.x_hi, me.y, low, me.x_lo, me.c]
    stage = [sender.start(line, line, me.along_y(k)[1]) for k in range(1, n_y)]
    line = full.at[me.x_hi, me.y, top, me.x_lo, me.c]
    stage += [sender.start(line, line, me.along_x(k)[1]) for k in range(1, n_x)]
    for copy in stage:
        copy.wait_recv()
    plane = full.at[me.x_hi, :, low, me.x_lo, me.c]
    stage = [sender.start(plane, plane, me.along_x(k)[1]) for k in range(1, n_x)]
    plane = full.at[:, me.y, top, :, me.c]
    stage += [sender.start(plane, plane, me.along_y(k)[1]) for k in range(1, n_y)]
    for copy in stage:
        copy.wait_recv()
    side = full.at[:, :, :, :, me.c]
    sender.start(side, side, me.partner()).wait_recv()


def gather_kernel(dims, own, full, send_sem, recv_sem, local_sem):
    me = Place(dims)
    me.meet()
    sender = Sender(send_sem, recv_sem)
    gather_rows(me, own, full, sender, local_sem)
    sender.finish()


def gather_hot(own, dims):
    count = copies_of_gather(dims)
    full = pl.pallas_call(
        functools.partial(gather_kernel, dims),
        out_shape=jax.ShapeDtypeStruct((*dims, *own.shape), own.dtype),
        in_specs=[pl.BlockSpec(memory_space=pltpu.VMEM)],
        out_specs=pl.BlockSpec(memory_space=pltpu.VMEM),
        scratch_shapes=[
            pltpu.SemaphoreType.DMA((count,)),
            pltpu.SemaphoreType.DMA((count,)),
            pltpu.SemaphoreType.DMA,
        ],
        compiler_params=pltpu.CompilerParams(collective_id=0, has_side_effects=True),
        name="gather_hot",
    )(own)
    return full.reshape(-1, own.shape[1])


def update_kernel(
    dims, part, old, grad, full,
    twin, packed, in_a, in_b, sum_a, sum_b, in_a2, in_b2, line, in_z, fresh,
    send_sem, recv_sem, local_sem,
):
    me = Place(dims)
    n_hi, n_y, n_z, n_lo, _ = dims
    n_x = n_hi * n_lo
    half = n_z // 2
    low, top = pl.ds(0, half), pl.ds(half, half)
    me.meet()
    sender = Sender(send_sem, recv_sem)
    f32, bf16 = jnp.float32, jnp.bfloat16

    sender.start(part.at[:, :, :, :, 1 - me.c], twin, me.partner()).wait_recv()

    def add_twin(i, carry):
        x_hi, y, z = i // (n_y * n_z), (i // n_z) % n_y, i % n_z
        for x_lo in range(n_lo):
            total = part[x_hi, y, z, x_lo, me.c] + twin[x_hi, y, z, x_lo]
            twin[x_hi, y, z, x_lo] = total
            packed[x_hi, y, z, x_lo] = total.astype(bf16)
        return carry

    lax.fori_loop(0, n_hi * n_y * n_z, add_twin, 0)

    stage = []
    for k in range(1, n_x):
        x, device = me.along_x(k)
        src = packed.at[x // n_lo, :, low, x % n_lo]
        stage.append(sender.start(src, in_a.at[k - 1], device))
    for k in range(1, n_y):
        y, device = me.along_y(k)
        stage.append(sender.start(packed.at[:, y, top], in_b.at[k - 1], device))
    for copy in stage:
        copy.wait_recv()

    def add_plane(z, carry):
        for y in range(n_y):
            total = twin[me.x_hi, y, z, me.x_lo]
            for k in range(n_x - 1):
                total = total + in_a[k, y, z].astype(f32)
            sum_a[y, z] = total
        for x_hi in range(n_hi):
            for x_lo in range(n_lo):
                total = twin[x_hi, me.y, half + z, x_lo]
                for k in range(n_y - 1):
                    total = total + in_b[k, x_hi, z, x_lo].astype(f32)
                sum_b[x_hi, x_lo, z] = total
        return carry

    lax.fori_loop(0, half, add_plane, 0)

    stage = []
    for k in range(1, n_y):
        y, device = me.along_y(k)
        stage.append(sender.start(sum_a.at[y], in_a2.at[k - 1], device))
    for k in range(1, n_x):
        x, device = me.along_x(k)
        stage.append(sender.start(sum_b.at[x // n_lo, x % n_lo], in_b2.at[k - 1], device))
    for copy in stage:
        copy.wait_recv()

    def add_line(z, carry):
        total = sum_a[me.y, z]
        for k in range(n_y - 1):
            total = total + in_a2[k, z]
        line[z] = total
        total = sum_b[me.x_hi, me.x_lo, z]
        for k in range(n_x - 1):
            total = total + in_b2[k, z]
        line[half + z] = total
        return carry

    lax.fori_loop(0, half, add_line, 0)

    stage = []
    for k in range(1, n_z):
        z, device = me.along_z(k)
        stage.append(sender.start(line.at[z], in_z.at[k - 1], device))
    for copy in stage:
        copy.wait_recv()
    total = line[me.z]
    for k in range(n_z - 1):
        total = total + in_z[k]
    grad[...] = total
    fresh[...] = (old[...] - 0.1 * total).astype(bf16)

    gather_rows(me, fresh, full, sender, local_sem)
    sender.finish()


def update_hot(part, old, dims):
    n_hi, n_y, n_z, n_lo, _ = dims
    n_x, half = n_hi * n_lo, n_z // 2
    tile = old.shape
    f32, bf16 = jnp.float32, jnp.bfloat16
    count = copies_of_gather(dims) + copies_of_scatter(dims)
    grad, full = pl.pallas_call(
        functools.partial(update_kernel, dims),
        out_shape=(
            jax.ShapeDtypeStruct(tile, f32),
            jax.ShapeDtypeStruct((*dims, *tile), bf16),
        ),
        in_specs=[pl.BlockSpec(memory_space=pltpu.VMEM)] * 2,
        out_specs=(pl.BlockSpec(memory_space=pltpu.VMEM),) * 2,
        scratch_shapes=[
            pltpu.VMEM((n_hi, n_y, n_z, n_lo, *tile), f32),
            pltpu.VMEM((n_hi, n_y, n_z, n_lo, *tile), bf16),
            pltpu.VMEM((n_x - 1, n_y, half, *tile), bf16),
            pltpu.VMEM((n_y - 1, n_hi, half, n_lo, *tile), bf16),
            pltpu.VMEM((n_y, half, *tile), f32),
            pltpu.VMEM((n_hi, n_lo, half, *tile), f32),
            pltpu.VMEM((n_y - 1, half, *tile), f32),
            pltpu.VMEM((n_x - 1, half, *tile), f32),
            pltpu.VMEM((n_z, *tile), f32),
            pltpu.VMEM((n_z - 1, *tile), f32),
            pltpu.VMEM(tile, bf16),
            pltpu.SemaphoreType.DMA((count,)),
            pltpu.SemaphoreType.DMA((count,)),
            pltpu.SemaphoreType.DMA,
        ],
        compiler_params=pltpu.CompilerParams(collective_id=1, has_side_effects=True),
        name="update_hot",
    )(part.reshape(*dims, *tile), old)
    return grad, full.reshape(-1, tile[1])


def body(dims, table, hot_slot, cold_row, cold_bag, hot_pick, dense, label):
    n = math.prod(dims)
    n_table, width = table.shape
    samples = dense.shape[0]
    own_hot = hot_slot.shape[0]
    cap = cold_row.shape[2]
    slots = cold_row.shape[1] * cap
    f32, bf16 = jnp.float32, jnp.bfloat16
    rounded = table.astype(bf16)

    arrived = exchange(cold_row[0]).reshape(slots)
    hot_old = table[hot_slot]
    hot_copy = gather_hot(hot_old.astype(bf16), dims)

    row_ids = jnp.arange(n_table, dtype=jnp.int32)
    at_row = (arrived[:, None] == row_ids[None, :]).astype(bf16)
    looked = jnp.dot(at_row, rounded, preferred_element_type=f32).astype(bf16)
    returned = exchange(looked.reshape(n, cap, width)).reshape(slots, width)

    bags = cold_bag[0].reshape(slots)
    sample_ids = jnp.arange(samples, dtype=jnp.int32)
    selector = (sample_ids[:, None] == bags[None, :]).astype(bf16)
    hot_ids = jnp.arange(n * own_hot, dtype=jnp.int32)
    counts = sum(
        (hot_pick[:, j][:, None] == hot_ids[None, :]).astype(f32)
        for j in range(hot_pick.shape[1])
    ).astype(bf16)
    counts = lax.optimization_barrier(counts)
    hot_pooled = jnp.dot(counts, hot_copy, preferred_element_type=f32)
    pooled = jnp.dot(selector, returned, preferred_element_type=f32) + hot_pooled
    score = jnp.sum(pooled * dense, axis=1) / width**0.5
    err = jax.nn.sigmoid(score) - label.astype(f32)
    grad = err[:, None] * dense
    high, low = split_bf16(grad)

    first = (((0,), (0,)), ((), ()))
    slot_grad = lax.dot_general(selector, high, first, preferred_element_type=f32).astype(bf16)
    delivered = exchange(slot_grad.reshape(n, cap, width)).reshape(slots, width)

    hot_local = lax.dot_general(counts, high, first, preferred_element_type=f32)
    hot_local = hot_local + lax.dot_general(counts, low, first, preferred_element_type=f32)
    own_grad, hot_new = update_hot(hot_local, hot_old, dims)

    table_grad = lax.dot_general(at_row, delivered, first, preferred_element_type=f32)
    at_hot = (row_ids[:, None] == hot_slot[None, :]).astype(f32)
    table_grad = table_grad + jnp.dot(
        at_hot, own_grad, precision=lax.Precision.HIGHEST, preferred_element_type=f32
    )
    new_table = table - 0.1 * table_grad
    return (pooled, new_table, hot_new.astype(f32))


def solution(mesh, dims=SHAPE):
    placed = (
        P(AXES, None),
        P(AXES),
        P(AXES, None, None),
        P(AXES, None, None),
        P(AXES, None),
        P(AXES, None),
        P(AXES),
    )
    return jax.shard_map(
        functools.partial(body, dims),
        mesh=mesh,
        in_specs=placed,
        out_specs=(P(AXES, None), P(AXES, None), P()),
        check_vma=False,
    )
```

```python
import functools
import math

import jax
import jax.numpy as jnp
from jax import lax
from jax.experimental import pallas as pl
from jax.experimental.pallas import tpu as pltpu
from jax.sharding import PartitionSpec as P

AXES = ("rows", "grp")
MESH = pl.DeviceIdType.MESH
SHAPE = (2, 4, 8, 2, 2)


def exchange(blocks):
    return lax.all_to_all(blocks, AXES, split_axis=0, concat_axis=0, tiled=True)


def split_bf16(value):
    high = lax.reduce_precision(value, exponent_bits=8, mantissa_bits=7)
    return high.astype(jnp.bfloat16), (value - high).astype(jnp.bfloat16)


class Place:
    def __init__(self, dims):
        self.dims = dims
        x_hi, y, z, x_lo, core = dims
        r, g = lax.axis_index("rows"), lax.axis_index("grp")
        self.x_hi, self.y, self.z = r // (y * z), (r // z) % y, r % z
        self.x_lo, self.c = g // core, g % core
        self.x = self.x_hi * x_lo + self.x_lo
        self.n = (x_hi * x_lo, y, z)

    def device(self, x, y, z, c):
        _, n_y, n_z, n_lo, n_core = self.dims
        return ((x // n_lo * n_y + y) * n_z + z, x % n_lo * n_core + c)

    def along_x(self, k):
        x = (self.x + k) % self.n[0]
        return x, self.device(x, self.y, self.z, self.c)

    def along_y(self, k):
        y = (self.y + k) % self.n[1]
        return y, self.device(self.x, y, self.z, self.c)

    def along_z(self, k):
        z = (self.z + k) % self.n[2]
        return z, self.device(self.x, self.y, z, self.c)

    def partner(self):
        return self.device(self.x, self.y, self.z, 1 - self.c)

    def meet(self):
        barrier = pltpu.get_barrier_semaphore()
        n_x, n_y, n_z = self.n
        peers = [self.along_z(k)[1] for k in range(1, n_z)]
        peers += [self.along_y(k)[1] for k in range(1, n_y)]
        peers += [self.along_x(k)[1] for k in range(1, n_x)]
        peers += [self.partner()]
        for peer in peers:
            pl.semaphore_signal(barrier, inc=1, device_id=peer, device_id_type=MESH)
        pl.semaphore_wait(barrier, len(peers))


class Sender:
    def __init__(self, send_sem, recv_sem):
        self.send_sem, self.recv_sem = send_sem, recv_sem
        self.used = 0
        self.all = []

    def start(self, src, dst, device):
        copy = pltpu.make_async_remote_copy(
            src_ref=src,
            dst_ref=dst,
            send_sem=self.send_sem.at[self.used],
            recv_sem=self.recv_sem.at[self.used],
            device_id=device,
            device_id_type=MESH,
        )
        copy.start()
        self.used += 1
        self.all.append(copy)
        return copy

    def finish(self):
        for copy in self.all:
            copy.wait_send()


def spread_lines(me, own, line, plane_a, plane_b, sender, near):
    n_x, n_y, n_z = me.n
    half = n_z // 2
    low, top = pl.ds(0, half), pl.ds(half, half)
    keep = near.start(own, line.at[me.z])
    stage = [sender.start(own, line.at[me.z], me.along_z(k)[1]) for k in range(1, n_z)]
    yield
    keep.wait()
    for copy in stage:
        copy.wait_recv()
    to_a, to_b = plane_a.at[me.y], plane_b.at[me.x_hi, :, me.x_lo]
    stage = [sender.start(line.at[low], to_a, me.along_y(k)[1]) for k in range(1, n_y)]
    stage += [sender.start(line.at[top], to_b, me.along_x(k)[1]) for k in range(1, n_x)]
    keep = [near.start(line.at[low], to_a), near.start(line.at[top], to_b)]
    yield
    for copy in keep:
        copy.wait()
    for copy in stage:
        copy.wait_recv()
    yield


def spread_planes(me, plane_a, plane_b, full, sender, near):
    n_x, n_y, n_z = me.n
    n_lo = me.dims[3]
    half = n_z // 2
    low, top = pl.ds(0, half), pl.ds(half, half)

    def of_x(x):
        return full.at[x // n_lo, :, low, x % n_lo, me.c]

    def of_y(y):
        return full.at[:, y, top, :, me.c]

    over_x = [sender.start(plane_a, of_x(me.x), me.along_x(k)[1]) for k in range(1, n_x)]
    over_y = [sender.start(plane_b, of_y(me.y), me.along_y(k)[1]) for k in range(1, n_y)]
    side = [
        sender.start(plane_a, of_x(me.x), me.partner()),
        sender.start(plane_b, of_y(me.y), me.partner()),
    ]
    keep = [near.start(plane_a, of_x(me.x)), near.start(plane_b, of_y(me.y))]
    arrivals = [(copy, of_x((me.x + n_x - k) % n_x)) for k, copy in enumerate(over_x, 1)]
    arrivals += [(copy, of_y((me.y + n_y - k) % n_y)) for k, copy in enumerate(over_y, 1)]
    for copy, landed in arrivals:
        copy.wait_recv()
        side.append(sender.start(landed, landed, me.partner()))
    for copy in keep:
        copy.wait()
    for copy in side:
        copy.wait_recv()


class Near:
    def __init__(self, sem):
        self.sem, self.used = sem, 0

    def start(self, src, dst):
        copy = pltpu.make_async_copy(src, dst, self.sem.at[self.used])
        copy.start()
        self.used += 1
        return copy


SEMS = [pltpu.SemaphoreType.DMA((64,)), pltpu.SemaphoreType.DMA((64,)), pltpu.SemaphoreType.DMA((8,))]
IN_VMEM = pl.BlockSpec(memory_space=pltpu.VMEM)


def request_kernel(
    dims, width, asks, own, got, plane_a, plane_b, from_z, from_y, line,
    send_sem, recv_sem, near_sem,
):
    me = Place(dims)
    n_x, n_y, n_z = me.n
    me.meet()
    sender, near = Sender(send_sem, recv_sem), Near(near_sem)

    keep = near.start(asks.at[me.z], from_z.at[me.z])
    stage = []
    for k in range(1, n_z):
        z, device = me.along_z(k)
        stage.append(sender.start(asks.at[z], from_z.at[me.z], device))
    lines = spread_lines(me, own, line, plane_a, plane_b, sender, near)
    next(lines)
    keep.wait()
    for copy in stage:
        copy.wait_recv()

    def of_y(y):
        return from_z.at[:, y * width // 128]

    keep = near.start(of_y(me.y), from_y.at[me.y])
    stage = []
    for k in range(1, n_y):
        y, device = me.along_y(k)
        stage.append(sender.start(of_y(y), from_y.at[me.y], device))
    next(lines)
    keep.wait()
    for copy in stage:
        copy.wait_recv()

    mine = got.at[me.c, me.x]
    keep = near.start(from_y, mine)
    stage = [sender.start(from_y, mine, me.along_x(k)[1]) for k in range(1, n_x)]
    keep.wait()
    for copy in stage:
        copy.wait_recv()
    side = sender.start(got.at[me.c], got.at[me.c], me.partner())
    next(lines)
    side.wait_recv()
    sender.finish()


def request_rows(rows, own, dims):
    n_hi, n_y, n_z, n_lo, n_core = dims
    n_x, half = n_hi * n_lo, n_z // 2
    cap = rows.shape[1]
    width = n_x * n_core * cap
    tiles = -(-n_y * width // 128)
    asks = rows.reshape(*dims, cap).transpose(2, 1, 0, 3, 4, 5).reshape(n_z, n_y * width)
    asks = jnp.pad(asks, ((0, 0), (0, tiles * 128 - n_y * width)))
    got, plane_a, plane_b = pl.pallas_call(
        functools.partial(request_kernel, dims, width),
        out_shape=(
            jax.ShapeDtypeStruct((n_core, n_x, n_y, n_z, 1, 128), jnp.int32),
            jax.ShapeDtypeStruct((n_y, half, *own.shape), own.dtype),
            jax.ShapeDtypeStruct((n_hi, half, n_lo, *own.shape), own.dtype),
        ),
        in_specs=[IN_VMEM] * 2,
        out_specs=(IN_VMEM,) * 3,
        scratch_shapes=[
            pltpu.VMEM((n_z, tiles, 1, 128), jnp.int32),
            pltpu.VMEM((n_y, n_z, 1, 128), jnp.int32),
            pltpu.VMEM((n_z, *own.shape), own.dtype),
            *SEMS,
        ],
        compiler_params=pltpu.CompilerParams(collective_id=0, has_side_effects=True),
        name="request_rows",
    )(asks.reshape(n_z, tiles, 1, 128), own)
    r, g = lax.axis_index("rows"), lax.axis_index("grp")
    y = lax.rem(lax.div(r, n_z), n_y)
    pair = lax.div(r, n_y * n_z) * (n_lo * n_core) + g
    lane = lax.rem(y * width, 128) + pair * cap
    got = lax.dynamic_slice_in_dim(got.reshape(-1, 128), lane, cap, axis=1)
    got = got.reshape(n_core, n_hi, n_lo, n_y, n_z, cap).transpose(1, 3, 4, 2, 0, 5)
    return got.reshape(-1), plane_a, plane_b


def finish_kernel(dims, plane_a, plane_b, full, send_sem, recv_sem, near_sem):
    me = Place(dims)
    me.meet()
    sender, near = Sender(send_sem, recv_sem), Near(near_sem)
    spread_planes(me, plane_a, plane_b, full, sender, near)
    sender.finish()


def finish_gather(plane_a, plane_b, dims):
    tile = plane_a.shape[-2:]
    full = pl.pallas_call(
        functools.partial(finish_kernel, dims),
        out_shape=jax.ShapeDtypeStruct((*dims, *tile), plane_a.dtype),
        in_specs=[IN_VMEM] * 2,
        out_specs=IN_VMEM,
        scratch_shapes=SEMS,
        compiler_params=pltpu.CompilerParams(collective_id=2, has_side_effects=True),
        name="finish_gather",
    )(plane_a, plane_b)
    return full.reshape(-1, tile[1])


def update_kernel(
    dims, part, old, grad, full,
    twin_a, twin_b, packed_a, packed_b, in_a, in_b, in_a2, in_b2,
    line, in_z, fresh, spread, plane_a, plane_b,
    send_sem, recv_sem, near_sem,
):
    me = Place(dims)
    n_hi, n_y, n_z, n_lo, _ = dims
    n_x = n_hi * n_lo
    half = n_z // 2
    low, top = pl.ds(0, half), pl.ds(half, half)
    me.meet()
    sender, near = Sender(send_sem, recv_sem), Near(near_sem)
    f32, bf16 = jnp.float32, jnp.bfloat16

    chunks = []
    for k in [*range(1, max(n_x, n_y)), 0]:
        if k < n_x:
            x = me.along_x(k)[0]
            src = part.at[x // n_lo, :, low, x % n_lo, 1 - me.c]
            chunks.append((True, k, sender.start(src, twin_a.at[k], me.partner())))
        if k < n_y:
            y = me.along_y(k)[0]
            src = part.at[:, y, top, :, 1 - me.c]
            chunks.append((False, k, sender.start(src, twin_b.at[k], me.partner())))

    stage = []
    for is_a, k, copy in chunks:
        copy.wait_recv()
        x, to_x = me.along_x(k)
        y, to_y = me.along_y(k)

        def add_a(z, carry):
            for j in range(n_y):
                total = part[x // n_lo, j, z, x % n_lo, me.c] + twin_a[k, j, z]
                if k:
                    packed_a[k - 1, j, z] = total.astype(bf16)
                else:
                    twin_a[k, j, z] = total
            return carry

        def add_b(z, carry):
            for i in range(n_hi):
                for j in range(n_lo):
                    total = part[i, y, half + z, j, me.c] + twin_b[k, i, z, j]
                    if k:
                        packed_b[k - 1, i, j, z] = total.astype(bf16)
                    else:
                        twin_b[k, i, z, j] = total
            return carry

        lax.fori_loop(0, half, add_a if is_a else add_b, 0)
        if k and is_a:
            stage.append(sender.start(packed_a.at[k - 1], in_a.at[k - 1], to_x))
        elif k:
            stage.append(sender.start(packed_b.at[k - 1], in_b.at[k - 1], to_y))
    for copy in stage:
        copy.wait_recv()

    def add_plane(z, carry):
        for j in range(n_y):
            total = twin_a[0, j, z]
            for k in range(n_x - 1):
                total = total + in_a[k, j, z].astype(f32)
            twin_a[0, j, z] = total
        for i in range(n_hi):
            for j in range(n_lo):
                total = twin_b[0, i, z, j]
                for k in range(n_y - 1):
                    total = total + in_b[k, i, j, z].astype(f32)
                twin_b[0, i, z, j] = total
        return carry

    lax.fori_loop(0, half, add_plane, 0)

    stage = []
    for k in range(1, n_y):
        y, device = me.along_y(k)
        stage.append(sender.start(twin_a.at[0, y], in_a2.at[k - 1], device))
    for k in range(1, n_x):
        x, device = me.along_x(k)
        src = twin_b.at[0, x // n_lo, :, x % n_lo]
        stage.append(sender.start(src, in_b2.at[k - 1], device))
    for copy in stage:
        copy.wait_recv()

    def add_line(z, carry):
        total = twin_a[0, me.y, z]
        for k in range(n_y - 1):
            total = total + in_a2[k, z]
        line[z] = total
        total = twin_b[0, me.x_hi, z, me.x_lo]
        for k in range(n_x - 1):
            total = total + in_b2[k, z]
        line[half + z] = total
        return carry

    lax.fori_loop(0, half, add_line, 0)

    stage = []
    for k in range(1, n_z):
        z, device = me.along_z(k)
        stage.append(sender.start(line.at[z], in_z.at[k - 1], device))
    for copy in stage:
        copy.wait_recv()
    total = line[me.z]
    for k in range(n_z - 1):
        total = total + in_z[k]
    grad[...] = total
    fresh[...] = (old[...] - 0.1 * total).astype(bf16)

    for _ in spread_lines(me, fresh, spread, plane_a, plane_b, sender, near):
        pass
    spread_planes(me, plane_a, plane_b, full, sender, near)
    sender.finish()


def update_hot(part, old, dims):
    n_hi, n_y, n_z, n_lo, _ = dims
    n_x, half = n_hi * n_lo, n_z // 2
    tile = old.shape
    f32, bf16 = jnp.float32, jnp.bfloat16
    grad, full = pl.pallas_call(
        functools.partial(update_kernel, dims),
        out_shape=(
            jax.ShapeDtypeStruct(tile, f32),
            jax.ShapeDtypeStruct((*dims, *tile), bf16),
        ),
        in_specs=[IN_VMEM] * 2,
        out_specs=(IN_VMEM,) * 2,
        scratch_shapes=[
            pltpu.VMEM((n_x, n_y, half, *tile), f32),
            pltpu.VMEM((n_y, n_hi, half, n_lo, *tile), f32),
            pltpu.VMEM((n_x - 1, n_y, half, *tile), bf16),
            pltpu.VMEM((n_y - 1, n_hi, n_lo, half, *tile), bf16),
            pltpu.VMEM((n_x - 1, n_y, half, *tile), bf16),
            pltpu.VMEM((n_y - 1, n_hi, n_lo, half, *tile), bf16),
            pltpu.VMEM((n_y - 1, half, *tile), f32),
            pltpu.VMEM((n_x - 1, half, *tile), f32),
            pltpu.VMEM((n_z, *tile), f32),
            pltpu.VMEM((n_z - 1, *tile), f32),
            pltpu.VMEM(tile, bf16),
            pltpu.VMEM((n_z, *tile), bf16),
            pltpu.VMEM((n_y, half, *tile), bf16),
            pltpu.VMEM((n_hi, half, n_lo, *tile), bf16),
            *SEMS,
        ],
        compiler_params=pltpu.CompilerParams(collective_id=1, has_side_effects=True),
        name="update_hot",
    )(part.reshape(*dims, *tile), old)
    return grad, full.reshape(-1, tile[1])


def body(dims, table, hot_slot, cold_row, cold_bag, hot_pick, dense, label):
    n = math.prod(dims)
    n_table, width = table.shape
    samples = dense.shape[0]
    own_hot = hot_slot.shape[0]
    cap = cold_row.shape[2]
    slots = cold_row.shape[1] * cap
    f32, bf16 = jnp.float32, jnp.bfloat16
    rounded = table.astype(bf16)

    hot_old = table[hot_slot]
    arrived, plane_a, plane_b = request_rows(cold_row[0], hot_old.astype(bf16), dims)

    row_ids = jnp.arange(n_table, dtype=jnp.int32)
    at_row = (arrived[:, None] == row_ids[None, :]).astype(bf16)
    looked = jnp.dot(at_row, rounded, preferred_element_type=f32).astype(bf16)
    returned = exchange(looked.reshape(n, cap, width)).reshape(slots, width)

    bags = cold_bag[0].reshape(slots)
    sample_ids = jnp.arange(samples, dtype=jnp.int32)
    selector = (sample_ids[:, None] == bags[None, :]).astype(bf16)
    hot_ids = jnp.arange(n * own_hot, dtype=jnp.int32)
    counts = sum(
        (hot_pick[:, j][:, None] == hot_ids[None, :]).astype(f32)
        for j in range(hot_pick.shape[1])
    ).astype(bf16)
    counts = lax.optimization_barrier(counts)
    hot_copy = finish_gather(plane_a, plane_b, dims)
    hot_pooled = jnp.dot(counts, hot_copy, preferred_element_type=f32)
    pooled = jnp.dot(selector, returned, preferred_element_type=f32) + hot_pooled
    score = jnp.sum(pooled * dense, axis=1) / width**0.5
    err = jax.nn.sigmoid(score) - label.astype(f32)
    grad = err[:, None] * dense
    high, low = split_bf16(grad)

    first = (((0,), (0,)), ((), ()))
    slot_grad = lax.dot_general(selector, high, first, preferred_element_type=f32).astype(bf16)
    delivered = exchange(slot_grad.reshape(n, cap, width)).reshape(slots, width)

    hot_local = lax.dot_general(counts, high, first, preferred_element_type=f32)
    hot_local = hot_local + lax.dot_general(counts, low, first, preferred_element_type=f32)
    own_grad, hot_new = update_hot(hot_local, hot_old, dims)

    table_grad = lax.dot_general(at_row, delivered, first, preferred_element_type=f32)
    at_hot = (row_ids[:, None] == hot_slot[None, :]).astype(f32)
    table_grad = table_grad + jnp.dot(
        at_hot, own_grad, precision=lax.Precision.HIGHEST, preferred_element_type=f32
    )
    new_table = table - 0.1 * table_grad
    return (pooled, new_table, hot_new.astype(f32))


def solution(mesh, dims=SHAPE):
    placed = (
        P(AXES, None),
        P(AXES),
        P(AXES, None, None),
        P(AXES, None, None),
        P(AXES, None),
        P(AXES, None),
        P(AXES),
    )
    return jax.shard_map(
        functools.partial(body, dims),
        mesh=mesh,
        in_specs=placed,
        out_specs=(P(AXES, None), P(AXES, None), P()),
        check_vma=False,
    )
```

```python
import functools
import math

import jax
import jax.numpy as jnp
from jax import lax
from jax.experimental import pallas as pl
from jax.experimental.pallas import tpu as pltpu
from jax.sharding import PartitionSpec as P

AXES = ("rows", "grp")
MESH = pl.DeviceIdType.MESH
SHAPE = (2, 4, 8, 2, 2)


def exchange(blocks):
    return lax.all_to_all(blocks, AXES, split_axis=0, concat_axis=0, tiled=True)


def split_bf16(value):
    high = lax.reduce_precision(value, exponent_bits=8, mantissa_bits=7)
    return high.astype(jnp.bfloat16), (value - high).astype(jnp.bfloat16)


class Place:
    def __init__(self, dims):
        self.dims = dims
        x_hi, y, z, x_lo, core = dims
        r, g = lax.axis_index("rows"), lax.axis_index("grp")
        self.x_hi, self.y, self.z = r // (y * z), (r // z) % y, r % z
        self.x_lo, self.c = g // core, g % core
        self.x = self.x_hi * x_lo + self.x_lo
        self.n = (x_hi * x_lo, y, z)

    def device(self, x, y, z, c):
        _, n_y, n_z, n_lo, n_core = self.dims
        return ((x // n_lo * n_y + y) * n_z + z, x % n_lo * n_core + c)

    def along_x(self, k):
        x = (self.x + k) % self.n[0]
        return x, self.device(x, self.y, self.z, self.c)

    def along_y(self, k):
        y = (self.y + k) % self.n[1]
        return y, self.device(self.x, y, self.z, self.c)

    def along_z(self, k):
        z = (self.z + k) % self.n[2]
        return z, self.device(self.x, self.y, z, self.c)

    def partner(self):
        return self.device(self.x, self.y, self.z, 1 - self.c)

    def meet(self):
        barrier = pltpu.get_barrier_semaphore()
        n_x, n_y, n_z = self.n
        peers = [self.along_z(k)[1] for k in range(1, n_z)]
        peers += [self.along_y(k)[1] for k in range(1, n_y)]
        peers += [self.along_x(k)[1] for k in range(1, n_x)]
        peers += [self.partner()]
        for peer in peers:
            pl.semaphore_signal(barrier, inc=1, device_id=peer, device_id_type=MESH)
        pl.semaphore_wait(barrier, len(peers))


class Sender:
    def __init__(self, send_sem, recv_sem):
        self.send_sem, self.recv_sem = send_sem, recv_sem
        self.used = 0
        self.all = []

    def start(self, src, dst, device):
        copy = pltpu.make_async_remote_copy(
            src_ref=src,
            dst_ref=dst,
            send_sem=self.send_sem.at[self.used],
            recv_sem=self.recv_sem.at[self.used],
            device_id=device,
            device_id_type=MESH,
        )
        copy.start()
        self.used += 1
        self.all.append(copy)
        return copy

    def finish(self):
        for copy in self.all:
            copy.wait_send()


def spread_lines(me, own, line, plane_a, plane_b, sender, near):
    n_x, n_y, n_z = me.n
    half = n_z // 2
    low, top = pl.ds(0, half), pl.ds(half, half)
    keep = near.start(own, line.at[me.z])
    stage = [sender.start(own, line.at[me.z], me.along_z(k)[1]) for k in range(1, n_z)]
    yield
    keep.wait()
    for copy in stage:
        copy.wait_recv()
    to_a, to_b = plane_a.at[me.y], plane_b.at[me.x_hi, :, me.x_lo]
    stage = [sender.start(line.at[low], to_a, me.along_y(k)[1]) for k in range(1, n_y)]
    stage += [sender.start(line.at[top], to_b, me.along_x(k)[1]) for k in range(1, n_x)]
    keep = [near.start(line.at[low], to_a), near.start(line.at[top], to_b)]
    yield
    for copy in keep:
        copy.wait()
    for copy in stage:
        copy.wait_recv()
    yield


def spread_planes(me, plane_a, plane_b, full, sender, near, meanwhile=tuple):
    n_x, n_y, n_z = me.n
    n_lo = me.dims[3]
    half = n_z // 2
    low, top = pl.ds(0, half), pl.ds(half, half)

    def of_x(x):
        return full.at[x // n_lo, :, low, x % n_lo, me.c]

    def of_y(y):
        return full.at[:, y, top, :, me.c]

    over_x = [sender.start(plane_a, of_x(me.x), me.along_x(k)[1]) for k in range(1, n_x)]
    over_y = [sender.start(plane_b, of_y(me.y), me.along_y(k)[1]) for k in range(1, n_y)]
    side = [
        sender.start(plane_a, of_x(me.x), me.partner()),
        sender.start(plane_b, of_y(me.y), me.partner()),
    ]
    keep = [near.start(plane_a, of_x(me.x)), near.start(plane_b, of_y(me.y))]
    arrivals = [(copy, of_x((me.x + n_x - k) % n_x)) for k, copy in enumerate(over_x, 1)]
    arrivals += [(copy, of_y((me.y + n_y - k) % n_y)) for k, copy in enumerate(over_y, 1)]
    result = meanwhile()
    for copy, landed in arrivals:
        copy.wait_recv()
        side.append(sender.start(landed, landed, me.partner()))
    for copy in keep:
        copy.wait()
    for copy in side:
        copy.wait_recv()
    return result


class Near:
    def __init__(self, sem):
        self.sem, self.used = sem, 0

    def start(self, src, dst):
        copy = pltpu.make_async_copy(src, dst, self.sem.at[self.used])
        copy.start()
        self.used += 1
        return copy


SEMS = [pltpu.SemaphoreType.DMA((96,)), pltpu.SemaphoreType.DMA((96,)), pltpu.SemaphoreType.DMA((16,))]
IN_VMEM = pl.BlockSpec(memory_space=pltpu.VMEM)


def request_kernel(
    dims, width, asks, table, slot, pick, got, plane_a, plane_b, old, counts,
    from_z, from_y, line, own,
    send_sem, recv_sem, near_sem,
):
    me = Place(dims)
    n_x, n_y, n_z = me.n
    for i in range(old.shape[0]):
        old[pl.ds(i, 1), :] = table[pl.ds(slot[i], 1), :]
    own[...] = old[...].astype(own.dtype)
    me.meet()
    sender, near = Sender(send_sem, recv_sem), Near(near_sem)

    keep = near.start(asks.at[me.z], from_z.at[me.z])
    stage = []
    for k in range(1, n_z):
        z, device = me.along_z(k)
        stage.append(sender.start(asks.at[z], from_z.at[me.z], device))
    lines = spread_lines(me, own, line, plane_a, plane_b, sender, near)
    next(lines)

    def count(i, carry):
        ids = i * 64 + lax.broadcasted_iota(jnp.int32, (64, pick.shape[1]), 0)
        total = jnp.zeros(ids.shape, jnp.float32)
        for j in range(pick.shape[0]):
            total = total + jnp.where(ids == pick[pl.ds(j, 1), :], 1.0, 0.0)
        counts[pl.ds(pl.multiple_of(i * 64, 64), 64), :] = total.astype(counts.dtype)
        return carry

    lax.fori_loop(0, counts.shape[0] // 64, count, 0)
    keep.wait()
    for copy in stage:
        copy.wait_recv()

    def of_y(y):
        return from_z.at[:, y * width // 128]

    keep = near.start(of_y(me.y), from_y.at[me.y])
    stage = []
    for k in range(1, n_y):
        y, device = me.along_y(k)
        stage.append(sender.start(of_y(y), from_y.at[me.y], device))
    next(lines)
    keep.wait()
    for copy in stage:
        copy.wait_recv()

    mine = got.at[me.c, me.x]
    keep = near.start(from_y, mine)
    stage = [sender.start(from_y, mine, me.along_x(k)[1]) for k in range(1, n_x)]
    keep.wait()
    for copy in stage:
        copy.wait_recv()
    side = sender.start(got.at[me.c], got.at[me.c], me.partner())
    next(lines)
    side.wait_recv()
    sender.finish()


def request_rows(rows, table, slot, pick, dims):
    n_hi, n_y, n_z, n_lo, n_core = dims
    n_x, half = n_hi * n_lo, n_z // 2
    cap = rows.shape[1]
    width = n_x * n_core * cap
    tiles = -(-n_y * width // 128)
    tile = (slot.shape[0], table.shape[1])
    bf16 = jnp.bfloat16
    asks = rows.reshape(*dims, cap).transpose(2, 1, 0, 3, 4, 5).reshape(n_z, n_y * width)
    asks = jnp.pad(asks, ((0, 0), (0, tiles * 128 - n_y * width)))
    got, plane_a, plane_b, old, counts = pl.pallas_call(
        functools.partial(request_kernel, dims, width),
        out_shape=(
            jax.ShapeDtypeStruct((n_core, n_x, n_y, n_z, 1, 128), jnp.int32),
            jax.ShapeDtypeStruct((n_y, half, *tile), bf16),
            jax.ShapeDtypeStruct((n_hi, half, n_lo, *tile), bf16),
            jax.ShapeDtypeStruct(tile, jnp.float32),
            jax.ShapeDtypeStruct((math.prod(dims) * tile[0], pick.shape[0]), bf16),
        ),
        in_specs=[IN_VMEM, IN_VMEM, pl.BlockSpec(memory_space=pltpu.SMEM), IN_VMEM],
        out_specs=(IN_VMEM,) * 5,
        scratch_shapes=[
            pltpu.VMEM((n_z, tiles, 1, 128), jnp.int32),
            pltpu.VMEM((n_y, n_z, 1, 128), jnp.int32),
            pltpu.VMEM((n_z, *tile), bf16),
            pltpu.VMEM(tile, bf16),
            *SEMS,
        ],
        compiler_params=pltpu.CompilerParams(collective_id=0, has_side_effects=True),
        name="request_rows",
    )(asks.reshape(n_z, tiles, 1, 128), table, slot, pick.T)
    r, g = lax.axis_index("rows"), lax.axis_index("grp")
    y = lax.rem(lax.div(r, n_z), n_y)
    pair = lax.div(r, n_y * n_z) * (n_lo * n_core) + g
    lane = lax.rem(y * width, 128) + pair * cap
    got = lax.dynamic_slice_in_dim(got.reshape(-1, 128), lane, cap, axis=1)
    return got.reshape(n_core, n_hi, n_lo, n_y, n_z, cap), plane_a, plane_b, old, counts


def finish_kernel(dims, plane_a, plane_b, full, send_sem, recv_sem, near_sem):
    me = Place(dims)
    me.meet()
    sender, near = Sender(send_sem, recv_sem), Near(near_sem)
    spread_planes(me, plane_a, plane_b, full, sender, near)
    sender.finish()


def finish_gather(plane_a, plane_b, dims):
    tile = plane_a.shape[-2:]
    full = pl.pallas_call(
        functools.partial(finish_kernel, dims),
        out_shape=jax.ShapeDtypeStruct((*dims, *tile), plane_a.dtype),
        in_specs=[IN_VMEM] * 2,
        out_specs=IN_VMEM,
        scratch_shapes=SEMS,
        compiler_params=pltpu.CompilerParams(collective_id=2, has_side_effects=True),
        name="finish_gather",
    )(plane_a, plane_b)
    return full.reshape(-1, tile[1])


def update_kernel(
    dims, part, old, slots, grad, full, cold,
    cold_z, cold_ya, cold_xa, cold_xb, cold_yb,
    twin_a, twin_b, packed_a, packed_b, in_a, in_b, in_a2, in_b2,
    line, in_z, fresh, spread, plane_a, plane_b,
    send_sem, recv_sem, near_sem,
):
    me = Place(dims)
    n_hi, n_y, n_z, n_lo, _ = dims
    n_x = n_hi * n_lo
    half = n_z // 2
    low, top = pl.ds(0, half), pl.ds(half, half)
    me.meet()
    sender, near = Sender(send_sem, recv_sem), Near(near_sem)
    f32, bf16 = jnp.float32, jnp.bfloat16

    keep_cold = near.start(slots.at[:, :, me.z], cold_z.at[me.z])
    cold_stage = []
    for k in range(1, n_z):
        z, device = me.along_z(k)
        cold_stage.append(sender.start(slots.at[:, :, z], cold_z.at[me.z], device))

    chunks = []
    for k in [*range(1, max(n_x, n_y)), 0]:
        if k < n_x:
            x = me.along_x(k)[0]
            src = part.at[x // n_lo, :, low, x % n_lo, 1 - me.c]
            chunks.append((True, k, sender.start(src, twin_a.at[k], me.partner())))
        if k < n_y:
            y = me.along_y(k)[0]
            src = part.at[:, y, top, :, 1 - me.c]
            chunks.append((False, k, sender.start(src, twin_b.at[k], me.partner())))

    stage = []
    for is_a, k, copy in chunks:
        copy.wait_recv()
        x, to_x = me.along_x(k)
        y, to_y = me.along_y(k)

        def add_a(z, carry):
            for j in range(n_y):
                total = part[x // n_lo, j, z, x % n_lo, me.c] + twin_a[k, j, z]
                if k:
                    packed_a[k - 1, j, z] = total.astype(bf16)
                else:
                    twin_a[k, j, z] = total
            return carry

        def add_b(z, carry):
            for i in range(n_hi):
                for j in range(n_lo):
                    total = part[i, y, half + z, j, me.c] + twin_b[k, i, z, j]
                    if k:
                        packed_b[k - 1, i, j, z] = total.astype(bf16)
                    else:
                        twin_b[k, i, z, j] = total
            return carry

        lax.fori_loop(0, half, add_a if is_a else add_b, 0)
        if k and is_a:
            stage.append(sender.start(packed_a.at[k - 1], in_a.at[k - 1], to_x))
        elif k:
            stage.append(sender.start(packed_b.at[k - 1], in_b.at[k - 1], to_y))
    for copy in stage:
        copy.wait_recv()

    def add_plane(z, carry):
        for j in range(n_y):
            total = twin_a[0, j, z]
            for k in range(n_x - 1):
                total = total + in_a[k, j, z].astype(f32)
            twin_a[0, j, z] = total
        for i in range(n_hi):
            for j in range(n_lo):
                total = twin_b[0, i, z, j]
                for k in range(n_y - 1):
                    total = total + in_b[k, i, j, z].astype(f32)
                twin_b[0, i, z, j] = total
        return carry

    lax.fori_loop(0, half, add_plane, 0)

    stage = []
    for k in range(1, n_y):
        y, device = me.along_y(k)
        stage.append(sender.start(twin_a.at[0, y], in_a2.at[k - 1], device))
    for k in range(1, n_x):
        x, device = me.along_x(k)
        src = twin_b.at[0, x // n_lo, :, x % n_lo]
        stage.append(sender.start(src, in_b2.at[k - 1], device))
    for copy in stage:
        copy.wait_recv()

    def add_line(z, carry):
        total = twin_a[0, me.y, z]
        for k in range(n_y - 1):
            total = total + in_a2[k, z]
        line[z] = total
        total = twin_b[0, me.x_hi, z, me.x_lo]
        for k in range(n_x - 1):
            total = total + in_b2[k, z]
        line[half + z] = total
        return carry

    lax.fori_loop(0, half, add_line, 0)

    stage = []
    for k in range(1, n_z):
        z, device = me.along_z(k)
        stage.append(sender.start(line.at[z], in_z.at[k - 1], device))

    keep_cold.wait()
    for copy in cold_stage:
        copy.wait_recv()

    def ya(y):
        return cold_z.at[low, :, y]

    def xb(x):
        return cold_z.at[top, x // n_lo, :, x % n_lo]

    keep_cold = [near.start(ya(me.y), cold_ya.at[me.y]), near.start(xb(me.x), cold_xb.at[me.x])]
    cold_stage = []
    for k in range(1, n_y):
        y, device = me.along_y(k)
        cold_stage.append(sender.start(ya(y), cold_ya.at[me.y], device))
    for k in range(1, n_x):
        x, device = me.along_x(k)
        cold_stage.append(sender.start(xb(x), cold_xb.at[me.x], device))

    for copy in stage:
        copy.wait_recv()
    total = line[me.z]
    for k in range(n_z - 1):
        total = total + in_z[k]
    grad[...] = total
    fresh[...] = (old[...] - 0.1 * total).astype(bf16)

    lines = spread_lines(me, fresh, spread, plane_a, plane_b, sender, near)
    next(lines)

    for copy in keep_cold:
        copy.wait()
    for copy in cold_stage:
        copy.wait_recv()

    def xa(x):
        return cold_ya.at[:, :, x // n_lo, x % n_lo]

    def yb(y):
        return cold_xb.at[:, :, y]

    keep_cold = [near.start(xa(me.x), cold_xa.at[me.x]), near.start(yb(me.y), cold_yb.at[:, me.y])]
    cold_stage = []
    for k in range(1, n_x):
        x, device = me.along_x(k)
        cold_stage.append(sender.start(xa(x), cold_xa.at[me.x], device))
    for k in range(1, n_y):
        y, device = me.along_y(k)
        cold_stage.append(sender.start(yb(y), cold_yb.at[:, me.y], device))

    next(lines)
    next(lines)

    def swap_cold():
        for copy in keep_cold:
            copy.wait()
        for copy in cold_stage:
            copy.wait_recv()
        pairs = [(cold_xa, cold.at[me.c, :, :, low]), (cold_yb, cold.at[me.c, :, :, top])]
        kept = [near.start(src.at[:, :, :, me.c], dst) for src, dst in pairs]
        sent = [sender.start(src.at[:, :, :, 1 - me.c], dst, me.partner()) for src, dst in pairs]
        return kept, sent

    kept, sent = spread_planes(me, plane_a, plane_b, full, sender, near, swap_cold)
    for copy in kept:
        copy.wait()
    for copy in sent:
        copy.wait_recv()
    sender.finish()


def update_hot(part, old, slots, dims):
    n_hi, n_y, n_z, n_lo, _ = dims
    n_x, half = n_hi * n_lo, n_z // 2
    tile = old.shape
    f32, bf16 = jnp.float32, jnp.bfloat16
    unit = slots.shape[-2:]
    n_core = dims[4]
    grad, full, cold = pl.pallas_call(
        functools.partial(update_kernel, dims),
        out_shape=(
            jax.ShapeDtypeStruct(tile, f32),
            jax.ShapeDtypeStruct((*dims, *tile), bf16),
            jax.ShapeDtypeStruct((n_core, n_x, n_y, n_z, *unit), bf16),
        ),
        in_specs=[IN_VMEM] * 3,
        out_specs=(IN_VMEM,) * 3,
        scratch_shapes=[
            pltpu.VMEM((n_z, n_hi, n_y, n_lo, n_core, *unit), bf16),
            pltpu.VMEM((n_y, half, n_hi, n_lo, n_core, *unit), bf16),
            pltpu.VMEM((n_x, n_y, half, n_core, *unit), bf16),
            pltpu.VMEM((n_x, half, n_y, n_core, *unit), bf16),
            pltpu.VMEM((n_x, n_y, half, n_core, *unit), bf16),
            pltpu.VMEM((n_x, n_y, half, *tile), f32),
            pltpu.VMEM((n_y, n_hi, half, n_lo, *tile), f32),
            pltpu.VMEM((n_x - 1, n_y, half, *tile), bf16),
            pltpu.VMEM((n_y - 1, n_hi, n_lo, half, *tile), bf16),
            pltpu.VMEM((n_x - 1, n_y, half, *tile), bf16),
            pltpu.VMEM((n_y - 1, n_hi, n_lo, half, *tile), bf16),
            pltpu.VMEM((n_y - 1, half, *tile), f32),
            pltpu.VMEM((n_x - 1, half, *tile), f32),
            pltpu.VMEM((n_z, *tile), f32),
            pltpu.VMEM((n_z - 1, *tile), f32),
            pltpu.VMEM(tile, bf16),
            pltpu.VMEM((n_z, *tile), bf16),
            pltpu.VMEM((n_y, half, *tile), bf16),
            pltpu.VMEM((n_hi, half, n_lo, *tile), bf16),
            *SEMS,
        ],
        compiler_params=pltpu.CompilerParams(collective_id=1, has_side_effects=True),
        name="update_hot",
    )(part.reshape(*dims, *tile), old, slots.reshape(*dims, *unit))
    return grad, full.reshape(-1, tile[1]), cold.reshape(-1, unit[1])


def body(dims, table, hot_slot, cold_row, cold_bag, hot_pick, dense, label):
    n = math.prod(dims)
    n_table, width = table.shape
    samples = dense.shape[0]
    cap = cold_row.shape[2]
    slots = cold_row.shape[1] * cap
    f32, bf16 = jnp.float32, jnp.bfloat16
    rounded = table.astype(bf16)

    asked, plane_a, plane_b, hot_old, counts = request_rows(
        cold_row[0], table, hot_slot, hot_pick, dims
    )
    arrived = asked.transpose(1, 3, 4, 2, 0, 5).reshape(slots)
    asked = asked.reshape(slots)

    row_ids = jnp.arange(n_table, dtype=jnp.int32)
    at_row = (arrived[:, None] == row_ids[None, :]).astype(bf16)
    looked = jnp.dot(at_row, rounded, preferred_element_type=f32).astype(bf16)
    returned = exchange(looked.reshape(n, cap, width)).reshape(slots, width)

    bags = cold_bag[0].reshape(slots)
    sample_ids = jnp.arange(samples, dtype=jnp.int32)
    selector = (sample_ids[:, None] == bags[None, :]).astype(bf16)
    hot_copy = finish_gather(plane_a, plane_b, dims)
    first = (((0,), (0,)), ((), ()))
    hot_pooled = lax.dot_general(counts, hot_copy, first, preferred_element_type=f32)
    pooled = jnp.dot(selector, returned, preferred_element_type=f32) + hot_pooled
    score = jnp.sum(pooled * dense, axis=1) / width**0.5
    err = jax.nn.sigmoid(score) - label.astype(f32)
    grad = err[:, None] * dense
    high, low = split_bf16(grad)

    slot_grad = lax.dot_general(selector, high, first, preferred_element_type=f32).astype(bf16)
    hot_local = jnp.dot(counts, high, preferred_element_type=f32)
    hot_local = hot_local + jnp.dot(counts, low, preferred_element_type=f32)
    own_grad, hot_new, delivered = update_hot(
        hot_local, hot_old, slot_grad.reshape(n, cap, width), dims
    )

    from_row = (row_ids[:, None] == asked[None, :]).astype(bf16)
    table_grad = jnp.dot(from_row, delivered, preferred_element_type=f32)
    at_hot = (row_ids[:, None] == hot_slot[None, :]).astype(f32)
    table_grad = table_grad + jnp.dot(
        at_hot, own_grad, precision=lax.Precision.HIGHEST, preferred_element_type=f32
    )
    new_table = table - 0.1 * table_grad
    return (pooled, new_table, hot_new.astype(f32))


def solution(mesh, dims=SHAPE):
    placed = (
        P(AXES, None),
        P(AXES),
        P(AXES, None, None),
        P(AXES, None, None),
        P(AXES, None),
        P(AXES, None),
        P(AXES),
    )
    return jax.shard_map(
        functools.partial(body, dims),
        mesh=mesh,
        in_specs=placed,
        out_specs=(P(AXES, None), P(AXES, None), P()),
        check_vma=False,
    )
```

```python
import functools
import math

import jax
import jax.numpy as jnp
from jax import lax
from jax.experimental import pallas as pl
from jax.experimental.pallas import tpu as pltpu
from jax.sharding import PartitionSpec as P

AXES = ("rows", "grp")
MESH = pl.DeviceIdType.MESH
SHAPE = (2, 4, 8, 2, 2)


def exchange(blocks):
    return lax.all_to_all(blocks, AXES, split_axis=0, concat_axis=0, tiled=True)


def split_bf16(value):
    high = lax.reduce_precision(value, exponent_bits=8, mantissa_bits=7)
    return high.astype(jnp.bfloat16), (value - high).astype(jnp.bfloat16)


class Place:
    def __init__(self, dims):
        self.dims = dims
        x_hi, y, z, x_lo, core = dims
        r, g = lax.axis_index("rows"), lax.axis_index("grp")
        self.x_hi, self.y, self.z = r // (y * z), (r // z) % y, r % z
        self.x_lo, self.c = g // core, g % core
        self.x = self.x_hi * x_lo + self.x_lo
        self.n = (x_hi * x_lo, y, z)

    def device(self, x, y, z, c):
        _, n_y, n_z, n_lo, n_core = self.dims
        return ((x // n_lo * n_y + y) * n_z + z, x % n_lo * n_core + c)

    def along_x(self, k):
        x = (self.x + k) % self.n[0]
        return x, self.device(x, self.y, self.z, self.c)

    def along_y(self, k):
        y = (self.y + k) % self.n[1]
        return y, self.device(self.x, y, self.z, self.c)

    def along_z(self, k):
        z = (self.z + k) % self.n[2]
        return z, self.device(self.x, self.y, z, self.c)

    def partner(self):
        return self.device(self.x, self.y, self.z, 1 - self.c)

    def greet(self):
        n_x, n_y, n_z = self.n
        peers = [self.along_z(k)[1] for k in range(1, n_z)]
        peers += [self.along_y(k)[1] for k in range(1, n_y)]
        peers += [self.along_x(k)[1] for k in range(1, n_x)]
        peers += [self.partner()]
        for peer in peers:
            pl.semaphore_signal(
                pltpu.get_barrier_semaphore(), inc=1, device_id=peer, device_id_type=MESH
            )

    def meet(self):
        pl.semaphore_wait(pltpu.get_barrier_semaphore(), sum(self.n) - 2)


class Sender:
    def __init__(self, send_sem, recv_sem):
        self.send_sem, self.recv_sem = send_sem, recv_sem
        self.used = 0
        self.all = []

    def start(self, src, dst, device):
        copy = pltpu.make_async_remote_copy(
            src_ref=src,
            dst_ref=dst,
            send_sem=self.send_sem.at[self.used],
            recv_sem=self.recv_sem.at[self.used],
            device_id=device,
            device_id_type=MESH,
        )
        copy.start()
        self.used += 1
        self.all.append(copy)
        return copy

    def finish(self):
        for copy in self.all:
            copy.wait_send()


def spread_lines(me, own, line, plane_a, plane_b, sender, near):
    n_x, n_y, n_z = me.n
    half = n_z // 2
    low, top = pl.ds(0, half), pl.ds(half, half)
    keep = near.start(own, line.at[me.z])
    stage = [sender.start(own, line.at[me.z], me.along_z(k)[1]) for k in range(1, n_z)]
    yield
    keep.wait()
    for copy in stage:
        copy.wait_recv()
    to_a, to_b = plane_a.at[me.y], plane_b.at[me.x_hi, :, me.x_lo]
    stage = [sender.start(line.at[low], to_a, me.along_y(k)[1]) for k in range(1, n_y)]
    stage += [sender.start(line.at[top], to_b, me.along_x(k)[1]) for k in range(1, n_x)]
    keep = [near.start(line.at[low], to_a), near.start(line.at[top], to_b)]
    yield
    for copy in keep:
        copy.wait()
    for copy in stage:
        copy.wait_recv()
    yield


def spread_planes(me, plane_a, plane_b, full, sender, near, meanwhile=tuple):
    n_x, n_y, n_z = me.n
    n_lo = me.dims[3]
    half = n_z // 2
    low, top = pl.ds(0, half), pl.ds(half, half)

    def of_x(x):
        return full.at[x // n_lo, :, low, x % n_lo, me.c]

    def of_y(y):
        return full.at[:, y, top, :, me.c]

    over_x = [sender.start(plane_a, of_x(me.x), me.along_x(k)[1]) for k in range(1, n_x)]
    over_y = [sender.start(plane_b, of_y(me.y), me.along_y(k)[1]) for k in range(1, n_y)]
    side = [
        sender.start(plane_a, of_x(me.x), me.partner()),
        sender.start(plane_b, of_y(me.y), me.partner()),
    ]
    keep = [near.start(plane_a, of_x(me.x)), near.start(plane_b, of_y(me.y))]
    arrivals = [(copy, of_x((me.x + n_x - k) % n_x)) for k, copy in enumerate(over_x, 1)]
    arrivals += [(copy, of_y((me.y + n_y - k) % n_y)) for k, copy in enumerate(over_y, 1)]
    result = meanwhile()
    for copy, landed in arrivals:
        copy.wait_recv()
        side.append(sender.start(landed, landed, me.partner()))
    for copy in keep:
        copy.wait()
    for copy in side:
        copy.wait_recv()
    return result


class Near:
    def __init__(self, sem):
        self.sem, self.used = sem, 0

    def start(self, src, dst):
        copy = pltpu.make_async_copy(src, dst, self.sem.at[self.used])
        copy.start()
        self.used += 1
        return copy


def semaphores(remote, near):
    dma = pltpu.SemaphoreType.DMA
    return [dma((remote,)), dma((remote,)), dma((near,))]


IN_VMEM = pl.BlockSpec(memory_space=pltpu.VMEM)


def request_kernel(
    dims, width, asks, table, slot, pick, got, plane_a, plane_b, old, counts,
    from_z, from_y, line, own,
    send_sem, recv_sem, near_sem,
):
    me = Place(dims)
    n_x, n_y, n_z = me.n
    me.greet()
    for i in range(old.shape[0]):
        old[pl.ds(i, 1), :] = table[pl.ds(slot[i], 1), :]
    own[...] = old[...].astype(own.dtype)

    def count(i, carry):
        ids = i * 64 + lax.broadcasted_iota(jnp.int32, (64, pick.shape[1]), 0)
        total = jnp.zeros(ids.shape, jnp.float32)
        for j in range(pick.shape[0]):
            total = total + jnp.where(ids == pick[pl.ds(j, 1), :], 1.0, 0.0)
        counts[pl.ds(pl.multiple_of(i * 64, 64), 64), :] = total.astype(counts.dtype)
        return carry

    pieces = counts.shape[0] // 64
    lax.fori_loop(0, pieces // 4, count, 0)
    me.meet()
    sender, near = Sender(send_sem, recv_sem), Near(near_sem)

    keep = near.start(asks.at[me.z], from_z.at[me.z])
    stage = []
    for k in range(1, n_z):
        z, device = me.along_z(k)
        stage.append(sender.start(asks.at[z], from_z.at[me.z], device))
    lines = spread_lines(me, own, line, plane_a, plane_b, sender, near)
    next(lines)

    lax.fori_loop(pieces // 4, pieces, count, 0)
    keep.wait()
    for copy in stage:
        copy.wait_recv()

    def of_y(y):
        return from_z.at[:, y * width // 128]

    keep = near.start(of_y(me.y), from_y.at[me.y])
    stage = []
    for k in range(1, n_y):
        y, device = me.along_y(k)
        stage.append(sender.start(of_y(y), from_y.at[me.y], device))
    next(lines)
    keep.wait()
    for copy in stage:
        copy.wait_recv()

    mine = got.at[me.c, me.x]
    keep = near.start(from_y, mine)
    stage = [sender.start(from_y, mine, me.along_x(k)[1]) for k in range(1, n_x)]
    keep.wait()
    for copy in stage:
        copy.wait_recv()
    side = sender.start(got.at[me.c], got.at[me.c], me.partner())
    next(lines)
    side.wait_recv()
    sender.finish()


def request_rows(rows, table, slot, pick, dims):
    n_hi, n_y, n_z, n_lo, n_core = dims
    n_x, half = n_hi * n_lo, n_z // 2
    cap = rows.shape[1]
    width = n_x * n_core * cap
    tiles = -(-n_y * width // 128)
    tile = (slot.shape[0], table.shape[1])
    bf16 = jnp.bfloat16
    asks = rows.reshape(*dims, cap).transpose(2, 1, 0, 3, 4, 5).reshape(n_z, n_y * width)
    asks = jnp.pad(asks, ((0, 0), (0, tiles * 128 - n_y * width)))
    got, plane_a, plane_b, old, counts = pl.pallas_call(
        functools.partial(request_kernel, dims, width),
        out_shape=(
            jax.ShapeDtypeStruct((n_core, n_x, n_y, n_z, 1, 128), jnp.int32),
            jax.ShapeDtypeStruct((n_y, half, *tile), bf16),
            jax.ShapeDtypeStruct((n_hi, half, n_lo, *tile), bf16),
            jax.ShapeDtypeStruct(tile, jnp.float32),
            jax.ShapeDtypeStruct((math.prod(dims) * tile[0], pick.shape[0]), bf16),
        ),
        in_specs=[IN_VMEM, IN_VMEM, pl.BlockSpec(memory_space=pltpu.SMEM), IN_VMEM],
        out_specs=(IN_VMEM,) * 5,
        scratch_shapes=[
            pltpu.VMEM((n_z, tiles, 1, 128), jnp.int32),
            pltpu.VMEM((n_y, n_z, 1, 128), jnp.int32),
            pltpu.VMEM((n_z, *tile), bf16),
            pltpu.VMEM(tile, bf16),
            *semaphores(2 * (n_x + n_y + n_z) - 5, 6),
        ],
        compiler_params=pltpu.CompilerParams(collective_id=0, has_side_effects=True),
        name="request_rows",
    )(asks.reshape(n_z, tiles, 1, 128), table, slot, pick.T)
    r, g = lax.axis_index("rows"), lax.axis_index("grp")
    y = lax.rem(lax.div(r, n_z), n_y)
    pair = lax.div(r, n_y * n_z) * (n_lo * n_core) + g
    lane = lax.rem(y * width, 128) + pair * cap
    got = lax.dynamic_slice_in_dim(got.reshape(-1, 128), lane, cap, axis=1)
    return got.reshape(n_core, n_hi, n_lo, n_y, n_z, cap), plane_a, plane_b, old, counts


def finish_kernel(dims, plane_a, plane_b, full, send_sem, recv_sem, near_sem):
    me = Place(dims)
    me.greet()
    me.meet()
    sender, near = Sender(send_sem, recv_sem), Near(near_sem)
    spread_planes(me, plane_a, plane_b, full, sender, near)
    sender.finish()


def finish_gather(plane_a, plane_b, dims):
    n_x, n_y = dims[0] * dims[3], dims[1]
    tile = plane_a.shape[-2:]
    full = pl.pallas_call(
        functools.partial(finish_kernel, dims),
        out_shape=jax.ShapeDtypeStruct((*dims, *tile), plane_a.dtype),
        in_specs=[IN_VMEM] * 2,
        out_specs=IN_VMEM,
        scratch_shapes=semaphores(2 * (n_x + n_y) - 2, 2),
        compiler_params=pltpu.CompilerParams(collective_id=2, has_side_effects=True),
        name="finish_gather",
    )(plane_a, plane_b)
    return full.reshape(-1, tile[1])


def update_kernel(
    dims, counts, high, rest, old, slots, grad, full, cold,
    part,
    cold_z, cold_ya, cold_xa, cold_xb, cold_yb,
    twin_a, twin_b, packed_a, packed_b, in_a, in_b, in_a2, in_b2,
    line, in_z, fresh, spread, plane_a, plane_b,
    send_sem, recv_sem, near_sem,
):
    me = Place(dims)
    n_hi, n_y, n_z, n_lo, _ = dims
    n_x = n_hi * n_lo
    half = n_z // 2
    low, top = pl.ds(0, half), pl.ds(half, half)
    f32, bf16 = jnp.float32, jnp.bfloat16
    me.greet()

    rows = counts.shape[0] // (n_hi * n_y * 2)

    def multiply(i, carry):
        some = counts[pl.ds(pl.multiple_of(i * rows, rows), rows), :]
        total = jnp.dot(some, high[...], preferred_element_type=f32)
        total = total + jnp.dot(some, rest[...], preferred_element_type=f32)
        x_hi, y, z = i // (2 * n_y), i // 2 % n_y, i % 2 * half
        shape = (half, *part.shape[3:])
        part[x_hi, y, pl.ds(z, half)] = total.reshape(shape)
        return carry

    lax.fori_loop(0, n_hi * n_y * 2, multiply, 0)
    me.meet()
    sender, near = Sender(send_sem, recv_sem), Near(near_sem)

    keep_cold = near.start(slots.at[:, :, me.z], cold_z.at[me.z])
    cold_stage = []
    for k in range(1, n_z):
        z, device = me.along_z(k)
        cold_stage.append(sender.start(slots.at[:, :, z], cold_z.at[me.z], device))

    chunks = []
    for k in [*range(1, max(n_x, n_y)), 0]:
        if k < n_x:
            x = me.along_x(k)[0]
            src = part.at[x // n_lo, :, low, x % n_lo, 1 - me.c]
            chunks.append((True, k, sender.start(src, twin_a.at[k], me.partner())))
        if k < n_y:
            y = me.along_y(k)[0]
            src = part.at[:, y, top, :, 1 - me.c]
            chunks.append((False, k, sender.start(src, twin_b.at[k], me.partner())))

    stage = []
    for is_a, k, copy in chunks:
        copy.wait_recv()
        x, to_x = me.along_x(k)
        y, to_y = me.along_y(k)

        def add_a(z, carry):
            for j in range(n_y):
                total = part[x // n_lo, j, z, x % n_lo, me.c] + twin_a[k, j, z]
                if k:
                    packed_a[k - 1, j, z] = total.astype(bf16)
                else:
                    twin_a[k, j, z] = total
            return carry

        def add_b(z, carry):
            for i in range(n_hi):
                for j in range(n_lo):
                    total = part[i, y, half + z, j, me.c] + twin_b[k, i, z, j]
                    if k:
                        packed_b[k - 1, i, j, z] = total.astype(bf16)
                    else:
                        twin_b[k, i, z, j] = total
            return carry

        lax.fori_loop(0, half, add_a if is_a else add_b, 0)
        if k and is_a:
            stage.append(sender.start(packed_a.at[k - 1], in_a.at[k - 1], to_x))
        elif k:
            stage.append(sender.start(packed_b.at[k - 1], in_b.at[k - 1], to_y))
    for copy in stage:
        copy.wait_recv()

    def add_plane(z, carry):
        for j in range(n_y):
            total = twin_a[0, j, z]
            for k in range(n_x - 1):
                total = total + in_a[k, j, z].astype(f32)
            twin_a[0, j, z] = total
        for i in range(n_hi):
            for j in range(n_lo):
                total = twin_b[0, i, z, j]
                for k in range(n_y - 1):
                    total = total + in_b[k, i, j, z].astype(f32)
                twin_b[0, i, z, j] = total
        return carry

    lax.fori_loop(0, half, add_plane, 0)

    stage = []
    for k in range(1, n_y):
        y, device = me.along_y(k)
        stage.append(sender.start(twin_a.at[0, y], in_a2.at[k - 1], device))
    for k in range(1, n_x):
        x, device = me.along_x(k)
        src = twin_b.at[0, x // n_lo, :, x % n_lo]
        stage.append(sender.start(src, in_b2.at[k - 1], device))
    for copy in stage:
        copy.wait_recv()

    def add_line(z, carry):
        total = twin_a[0, me.y, z]
        for k in range(n_y - 1):
            total = total + in_a2[k, z]
        line[z] = total
        total = twin_b[0, me.x_hi, z, me.x_lo]
        for k in range(n_x - 1):
            total = total + in_b2[k, z]
        line[half + z] = total
        return carry

    lax.fori_loop(0, half, add_line, 0)

    stage = []
    for k in range(1, n_z):
        z, device = me.along_z(k)
        stage.append(sender.start(line.at[z], in_z.at[k - 1], device))

    for copy in stage:
        copy.wait_recv()
    total = line[me.z]
    for k in range(n_z - 1):
        total = total + in_z[k]
    grad[...] = total
    fresh[...] = (old[...] - 0.1 * total).astype(bf16)

    lines = spread_lines(me, fresh, spread, plane_a, plane_b, sender, near)
    next(lines)

    keep_cold.wait()
    for copy in cold_stage:
        copy.wait_recv()

    def ya(y):
        return cold_z.at[low, :, y]

    def xb(x):
        return cold_z.at[top, x // n_lo, :, x % n_lo]

    keep_cold = [near.start(ya(me.y), cold_ya.at[me.y]), near.start(xb(me.x), cold_xb.at[me.x])]
    cold_stage = []
    for k in range(1, n_y):
        y, device = me.along_y(k)
        cold_stage.append(sender.start(ya(y), cold_ya.at[me.y], device))
    for k in range(1, n_x):
        x, device = me.along_x(k)
        cold_stage.append(sender.start(xb(x), cold_xb.at[me.x], device))

    next(lines)
    next(lines)

    def turn_cold():
        for copy in keep_cold:
            copy.wait()
        for copy in cold_stage:
            copy.wait_recv()

        def xa(x):
            return cold_ya.at[:, :, x // n_lo, x % n_lo]

        def yb(y):
            return cold_xb.at[:, :, y]

        kept = [near.start(xa(me.x), cold_xa.at[me.x]), near.start(yb(me.y), cold_yb.at[:, me.y])]
        sent = []
        for k in range(1, n_x):
            x, device = me.along_x(k)
            sent.append(sender.start(xa(x), cold_xa.at[me.x], device))
        for k in range(1, n_y):
            y, device = me.along_y(k)
            sent.append(sender.start(yb(y), cold_yb.at[:, me.y], device))
        return kept, sent

    kept, sent = spread_planes(me, plane_a, plane_b, full, sender, near, turn_cold)
    for copy in kept:
        copy.wait()
    for copy in sent:
        copy.wait_recv()
    pairs = [(cold_xa, cold.at[me.c, :, :, low]), (cold_yb, cold.at[me.c, :, :, top])]
    kept = [near.start(src.at[:, :, :, me.c], dst) for src, dst in pairs]
    sent = [sender.start(src.at[:, :, :, 1 - me.c], dst, me.partner()) for src, dst in pairs]
    for copy in kept:
        copy.wait()
    for copy in sent:
        copy.wait_recv()
    sender.finish()


def update_hot(counts, high, rest, old, slots, dims):
    n_hi, n_y, n_z, n_lo, _ = dims
    n_x, half = n_hi * n_lo, n_z // 2
    tile = old.shape
    f32, bf16 = jnp.float32, jnp.bfloat16
    unit = slots.shape[-2:]
    n_core = dims[4]
    grad, full, cold = pl.pallas_call(
        functools.partial(update_kernel, dims),
        out_shape=(
            jax.ShapeDtypeStruct(tile, f32),
            jax.ShapeDtypeStruct((*dims, *tile), bf16),
            jax.ShapeDtypeStruct((n_core, n_x, n_y, n_z, *unit), bf16),
        ),
        in_specs=[IN_VMEM] * 5,
        out_specs=(IN_VMEM,) * 3,
        scratch_shapes=[
            pltpu.VMEM((*dims, *tile), f32),
            pltpu.VMEM((n_z, n_hi, n_y, n_lo, n_core, *unit), bf16),
            pltpu.VMEM((n_y, half, n_hi, n_lo, n_core, *unit), bf16),
            pltpu.VMEM((n_x, n_y, half, n_core, *unit), bf16),
            pltpu.VMEM((n_x, half, n_y, n_core, *unit), bf16),
            pltpu.VMEM((n_x, n_y, half, n_core, *unit), bf16),
            pltpu.VMEM((n_x, n_y, half, *tile), f32),
            pltpu.VMEM((n_y, n_hi, half, n_lo, *tile), f32),
            pltpu.VMEM((n_x - 1, n_y, half, *tile), bf16),
            pltpu.VMEM((n_y - 1, n_hi, n_lo, half, *tile), bf16),
            pltpu.VMEM((n_x - 1, n_y, half, *tile), bf16),
            pltpu.VMEM((n_y - 1, n_hi, n_lo, half, *tile), bf16),
            pltpu.VMEM((n_y - 1, half, *tile), f32),
            pltpu.VMEM((n_x - 1, half, *tile), f32),
            pltpu.VMEM((n_z, *tile), f32),
            pltpu.VMEM((n_z - 1, *tile), f32),
            pltpu.VMEM(tile, bf16),
            pltpu.VMEM((n_z, *tile), bf16),
            pltpu.VMEM((n_y, half, *tile), bf16),
            pltpu.VMEM((n_hi, half, n_lo, *tile), bf16),
            *semaphores(8 * (n_x + n_y) + 3 * n_z - 13, 12),
        ],
        compiler_params=pltpu.CompilerParams(collective_id=1, has_side_effects=True),
        name="update_hot",
    )(counts, high, rest, old, slots.reshape(*dims, *unit))
    return grad, full.reshape(-1, tile[1]), cold.reshape(-1, unit[1])


def body(dims, table, hot_slot, cold_row, cold_bag, hot_pick, dense, label):
    n = math.prod(dims)
    n_table, width = table.shape
    samples = dense.shape[0]
    cap = cold_row.shape[2]
    slots = cold_row.shape[1] * cap
    f32, bf16 = jnp.float32, jnp.bfloat16
    rounded = table.astype(bf16)

    asked, plane_a, plane_b, hot_old, counts = request_rows(
        cold_row[0], table, hot_slot, hot_pick, dims
    )
    arrived = asked.transpose(1, 3, 4, 2, 0, 5).reshape(slots)
    asked = asked.reshape(slots)

    row_ids = jnp.arange(n_table, dtype=jnp.int32)
    at_row = (arrived[:, None] == row_ids[None, :]).astype(bf16)
    looked = jnp.dot(at_row, rounded, preferred_element_type=f32).astype(bf16)
    returned = exchange(looked.reshape(n, cap, width)).reshape(slots, width)

    bags = cold_bag[0].reshape(slots)
    sample_ids = jnp.arange(samples, dtype=jnp.int32)
    selector = (sample_ids[:, None] == bags[None, :]).astype(bf16)
    hot_copy = finish_gather(plane_a, plane_b, dims)
    first = (((0,), (0,)), ((), ()))
    hot_pooled = lax.dot_general(counts, hot_copy, first, preferred_element_type=f32)
    pooled = jnp.dot(selector, returned, preferred_element_type=f32) + hot_pooled
    score = jnp.sum(pooled * dense, axis=1) / width**0.5
    err = jax.nn.sigmoid(score) - label.astype(f32)
    grad = err[:, None] * dense
    high, rest = split_bf16(grad)

    slot_grad = lax.dot_general(selector, high, first, preferred_element_type=f32).astype(bf16)
    own_grad, hot_new, delivered = update_hot(
        counts, high, rest, hot_old, slot_grad.reshape(n, cap, width), dims
    )

    from_row = (row_ids[:, None] == asked[None, :]).astype(bf16)
    table_grad = jnp.dot(from_row, delivered, preferred_element_type=f32)
    at_hot = (row_ids[:, None] == hot_slot[None, :]).astype(f32)
    table_grad = table_grad + jnp.dot(
        at_hot, own_grad, precision=lax.Precision.HIGHEST, preferred_element_type=f32
    )
    new_table = table - 0.1 * table_grad
    return (pooled, new_table, hot_new.astype(f32))


def solution(mesh, dims=SHAPE):
    placed = (
        P(AXES, None),
        P(AXES),
        P(AXES, None, None),
        P(AXES, None, None),
        P(AXES, None),
        P(AXES, None),
        P(AXES),
    )
    return jax.shard_map(
        functools.partial(body, dims),
        mesh=mesh,
        in_specs=placed,
        out_specs=(P(AXES, None), P(AXES, None), P()),
        check_vma=False,
    )
```

```python
import functools
import math

import jax
import jax.numpy as jnp
from jax import lax
from jax.experimental import pallas as pl
from jax.experimental.pallas import tpu as pltpu
from jax.sharding import PartitionSpec as P

AXES = ("rows", "grp")
MESH = pl.DeviceIdType.MESH
SHAPE = (2, 4, 8, 2, 2)


def exchange(blocks):
    return lax.all_to_all(blocks, AXES, split_axis=0, concat_axis=0, tiled=True)


def split_bf16(value):
    high = lax.reduce_precision(value, exponent_bits=8, mantissa_bits=7)
    return high.astype(jnp.bfloat16), (value - high).astype(jnp.bfloat16)


class Place:
    def __init__(self, dims):
        self.dims = dims
        x_hi, y, z, x_lo, core = dims
        r, g = lax.axis_index("rows"), lax.axis_index("grp")
        self.x_hi, self.y, self.z = r // (y * z), (r // z) % y, r % z
        self.x_lo, self.c = g // core, g % core
        self.x = self.x_hi * x_lo + self.x_lo
        self.n = (x_hi * x_lo, y, z)

    def device(self, x, y, z, c):
        _, n_y, n_z, n_lo, n_core = self.dims
        return ((x // n_lo * n_y + y) * n_z + z, x % n_lo * n_core + c)

    def along_x(self, k):
        x = (self.x + k) % self.n[0]
        return x, self.device(x, self.y, self.z, self.c)

    def along_y(self, k):
        y = (self.y + k) % self.n[1]
        return y, self.device(self.x, y, self.z, self.c)

    def along_z(self, k):
        z = (self.z + k) % self.n[2]
        return z, self.device(self.x, self.y, z, self.c)

    def partner(self):
        return self.device(self.x, self.y, self.z, 1 - self.c)

    def greet(self):
        n_x, n_y, n_z = self.n
        peers = [self.along_z(k)[1] for k in range(1, n_z)]
        peers += [self.along_y(k)[1] for k in range(1, n_y)]
        peers += [self.along_x(k)[1] for k in range(1, n_x)]
        peers += [self.partner()]
        for peer in peers:
            pl.semaphore_signal(
                pltpu.get_barrier_semaphore(), inc=1, device_id=peer, device_id_type=MESH
            )

    def meet(self):
        pl.semaphore_wait(pltpu.get_barrier_semaphore(), sum(self.n) - 2)


class Sender:
    def __init__(self, send_sem, recv_sem):
        self.send_sem, self.recv_sem = send_sem, recv_sem
        self.used = 0
        self.all = []

    def start(self, src, dst, device):
        copy = pltpu.make_async_remote_copy(
            src_ref=src,
            dst_ref=dst,
            send_sem=self.send_sem.at[self.used],
            recv_sem=self.recv_sem.at[self.used],
            device_id=device,
            device_id_type=MESH,
        )
        copy.start()
        self.used += 1
        self.all.append(copy)
        return copy

    def finish(self):
        for copy in self.all:
            copy.wait_send()


def spread_lines(me, own, line, plane_a, plane_b, sender, near):
    n_x, n_y, n_z = me.n
    half = n_z // 2
    low, top = pl.ds(0, half), pl.ds(half, half)
    keep = near.start(own, line.at[me.z])
    stage = [sender.start(own, line.at[me.z], me.along_z(k)[1]) for k in range(1, n_z)]
    yield
    keep.wait()
    for copy in stage:
        copy.wait_recv()
    to_a, to_b = plane_a.at[me.y], plane_b.at[me.x_hi, :, me.x_lo]
    stage = [sender.start(line.at[low], to_a, me.along_y(k)[1]) for k in range(1, n_y)]
    stage += [sender.start(line.at[top], to_b, me.along_x(k)[1]) for k in range(1, n_x)]
    keep = [near.start(line.at[low], to_a), near.start(line.at[top], to_b)]
    yield
    for copy in keep:
        copy.wait()
    for copy in stage:
        copy.wait_recv()
    yield


def spread_planes(me, plane_a, plane_b, full, sender, near, meanwhile=tuple):
    n_x, n_y, n_z = me.n
    n_lo = me.dims[3]
    half = n_z // 2
    low, top = pl.ds(0, half), pl.ds(half, half)

    def of_x(x):
        return full.at[x // n_lo, :, low, x % n_lo, me.c]

    def of_y(y):
        return full.at[:, y, top, :, me.c]

    over_x = [sender.start(plane_a, of_x(me.x), me.along_x(k)[1]) for k in range(1, n_x)]
    over_y = [sender.start(plane_b, of_y(me.y), me.along_y(k)[1]) for k in range(1, n_y)]
    side = [
        sender.start(plane_a, of_x(me.x), me.partner()),
        sender.start(plane_b, of_y(me.y), me.partner()),
    ]
    keep = [near.start(plane_a, of_x(me.x)), near.start(plane_b, of_y(me.y))]
    arrivals = [(copy, of_x((me.x + n_x - k) % n_x)) for k, copy in enumerate(over_x, 1)]
    arrivals += [(copy, of_y((me.y + n_y - k) % n_y)) for k, copy in enumerate(over_y, 1)]
    result = meanwhile()
    for copy, landed in arrivals:
        copy.wait_recv()
        side.append(sender.start(landed, landed, me.partner()))
    for copy in keep:
        copy.wait()
    for copy in side:
        copy.wait_recv()
    return result


class Near:
    def __init__(self, sem):
        self.sem, self.used = sem, 0

    def start(self, src, dst):
        copy = pltpu.make_async_copy(src, dst, self.sem.at[self.used])
        copy.start()
        self.used += 1
        return copy


def semaphores(remote, near):
    dma = pltpu.SemaphoreType.DMA
    return [dma((remote,)), dma((remote,)), dma((near,))]


IN_VMEM = pl.BlockSpec(memory_space=pltpu.VMEM)


def request_kernel(
    dims, width, asks, table, slot, pick, got, plane_a, plane_b, old, counts,
    from_z, from_y, line, own,
    send_sem, recv_sem, near_sem,
):
    me = Place(dims)
    n_x, n_y, n_z = me.n
    me.greet()
    for i in range(old.shape[0]):
        old[pl.ds(i, 1), :] = table[pl.ds(slot[i], 1), :]
    own[...] = old[...].astype(own.dtype)

    def count(i, carry):
        ids = i * 64 + lax.broadcasted_iota(jnp.int32, (64, pick.shape[1]), 0)
        total = jnp.zeros(ids.shape, jnp.float32)
        for j in range(pick.shape[0]):
            total = total + jnp.where(ids == pick[pl.ds(j, 1), :], 1.0, 0.0)
        counts[pl.ds(pl.multiple_of(i * 64, 64), 64), :] = total.astype(counts.dtype)
        return carry

    pieces = counts.shape[0] // 64
    lax.fori_loop(0, pieces // 4, count, 0)
    me.meet()
    sender, near = Sender(send_sem, recv_sem), Near(near_sem)

    keep = near.start(asks.at[me.z], from_z.at[me.z])
    stage = []
    for k in range(1, n_z):
        z, device = me.along_z(k)
        stage.append(sender.start(asks.at[z], from_z.at[me.z], device))
    lines = spread_lines(me, own, line, plane_a, plane_b, sender, near)
    next(lines)

    lax.fori_loop(pieces // 4, pieces, count, 0)
    keep.wait()
    for copy in stage:
        copy.wait_recv()

    def of_y(y):
        return from_z.at[:, y * width // 128]

    keep = near.start(of_y(me.y), from_y.at[me.y])
    stage = []
    for k in range(1, n_y):
        y, device = me.along_y(k)
        stage.append(sender.start(of_y(y), from_y.at[me.y], device))
    next(lines)
    keep.wait()
    for copy in stage:
        copy.wait_recv()

    mine = got.at[me.c, me.x]
    keep = near.start(from_y, mine)
    stage = [sender.start(from_y, mine, me.along_x(k)[1]) for k in range(1, n_x)]
    keep.wait()
    for copy in stage:
        copy.wait_recv()
    side = sender.start(got.at[me.c], got.at[me.c], me.partner())
    next(lines)
    side.wait_recv()
    sender.finish()


def request_rows(rows, table, slot, pick, dims):
    n_hi, n_y, n_z, n_lo, n_core = dims
    n_x, half = n_hi * n_lo, n_z // 2
    cap = rows.shape[1]
    width = n_x * n_core * cap
    tiles = -(-n_y * width // 128)
    tile = (slot.shape[0], table.shape[1])
    bf16 = jnp.bfloat16
    asks = rows.reshape(*dims, cap).transpose(2, 1, 0, 3, 4, 5).reshape(n_z, n_y * width)
    asks = jnp.pad(asks, ((0, 0), (0, tiles * 128 - n_y * width)))
    got, plane_a, plane_b, old, counts = pl.pallas_call(
        functools.partial(request_kernel, dims, width),
        out_shape=(
            jax.ShapeDtypeStruct((n_core, n_x, n_y, n_z, 1, 128), jnp.int32),
            jax.ShapeDtypeStruct((n_y, half, *tile), bf16),
            jax.ShapeDtypeStruct((n_hi, half, n_lo, *tile), bf16),
            jax.ShapeDtypeStruct(tile, jnp.float32),
            jax.ShapeDtypeStruct((math.prod(dims) * tile[0], pick.shape[0]), bf16),
        ),
        in_specs=[IN_VMEM, IN_VMEM, pl.BlockSpec(memory_space=pltpu.SMEM), IN_VMEM],
        out_specs=(IN_VMEM,) * 5,
        scratch_shapes=[
            pltpu.VMEM((n_z, tiles, 1, 128), jnp.int32),
            pltpu.VMEM((n_y, n_z, 1, 128), jnp.int32),
            pltpu.VMEM((n_z, *tile), bf16),
            pltpu.VMEM(tile, bf16),
            *semaphores(2 * (n_x + n_y + n_z) - 5, 6),
        ],
        compiler_params=pltpu.CompilerParams(collective_id=0, has_side_effects=True),
        name="request_rows",
    )(asks.reshape(n_z, tiles, 1, 128), table, slot, pick.T)
    r, g = lax.axis_index("rows"), lax.axis_index("grp")
    y = lax.rem(lax.div(r, n_z), n_y)
    pair = lax.div(r, n_y * n_z) * (n_lo * n_core) + g
    lane = lax.rem(y * width, 128) + pair * cap
    got = lax.dynamic_slice_in_dim(got.reshape(-1, 128), lane, cap, axis=1)
    return got.reshape(n_core, n_hi, n_lo, n_y, n_z, cap), plane_a, plane_b, old, counts


def finish_kernel(dims, plane_a, plane_b, full, send_sem, recv_sem, near_sem):
    me = Place(dims)
    me.greet()
    me.meet()
    sender, near = Sender(send_sem, recv_sem), Near(near_sem)
    spread_planes(me, plane_a, plane_b, full, sender, near)
    sender.finish()


def finish_gather(plane_a, plane_b, dims):
    n_x, n_y = dims[0] * dims[3], dims[1]
    tile = plane_a.shape[-2:]
    full = pl.pallas_call(
        functools.partial(finish_kernel, dims),
        out_shape=jax.ShapeDtypeStruct((*dims, *tile), plane_a.dtype),
        in_specs=[IN_VMEM] * 2,
        out_specs=IN_VMEM,
        scratch_shapes=semaphores(2 * (n_x + n_y) - 2, 2),
        compiler_params=pltpu.CompilerParams(collective_id=2, has_side_effects=True),
        name="finish_gather",
    )(plane_a, plane_b)
    return full.reshape(-1, tile[1])


def update_kernel(
    dims, counts, high, rest, old, slots, grad, full, cold,
    part,
    cold_z, cold_ya, cold_xa, cold_xb, cold_yb,
    twin_a, twin_b, packed_a, packed_b, in_a, in_b, in_a2, in_b2,
    line, in_z, fresh, spread, plane_a, plane_b,
    send_sem, recv_sem, near_sem,
):
    me = Place(dims)
    n_hi, n_y, n_z, n_lo, _ = dims
    n_x = n_hi * n_lo
    half = n_z // 2
    low, top = pl.ds(0, half), pl.ds(half, half)
    f32, bf16 = jnp.float32, jnp.bfloat16
    me.greet()

    rows = counts.shape[0] // (n_hi * n_y * 2)

    def multiply(i, carry):
        some = counts[pl.ds(pl.multiple_of(i * rows, rows), rows), :]
        total = jnp.dot(some, high[...], preferred_element_type=f32)
        total = total + jnp.dot(some, rest[...], preferred_element_type=f32)
        x_hi, y, z = i // (2 * n_y), i // 2 % n_y, i % 2 * half
        shape = (half, *part.shape[3:])
        part[x_hi, y, pl.ds(z, half)] = total.reshape(shape)
        return carry

    lax.fori_loop(0, n_hi * n_y * 2, multiply, 0)
    me.meet()
    sender, near = Sender(send_sem, recv_sem), Near(near_sem)

    near_first = sorted(range(1, n_z), key=lambda k: min(k, n_z - k))
    cold_in = {0: near.start(slots.at[:, :, me.z], cold_z.at[0])}
    for k in near_first:
        z, device = me.along_z(k)
        cold_in[k] = sender.start(slots.at[:, :, z], cold_z.at[k], device)
    kept, sent = [], []

    def turn_cold(k):
        if k:
            cold_in[k].wait_recv()
        else:
            cold_in[k].wait()
        if k < half:
            for j in range(n_y):
                y, device = me.along_y(j)
                src, dst = cold_z.at[k, :, y], cold_ya.at[me.y, k]
                if j:
                    sent.append(sender.start(src, dst, device))
                else:
                    kept.append(near.start(src, dst))
        else:
            for j in range(n_x):
                x, device = me.along_x(j)
                src, dst = cold_z.at[k, x // n_lo, :, x % n_lo], cold_xb.at[me.x, k - half]
                if j:
                    sent.append(sender.start(src, dst, device))
                else:
                    kept.append(near.start(src, dst))

    early = [0, *near_first[: n_z // 2]]

    chunks = []
    for k in [*range(1, max(n_x, n_y)), 0]:
        if k < n_x:
            x = me.along_x(k)[0]
            src = part.at[x // n_lo, :, low, x % n_lo, 1 - me.c]
            chunks.append((True, k, sender.start(src, twin_a.at[k], me.partner())))
        if k < n_y:
            y = me.along_y(k)[0]
            src = part.at[:, y, top, :, 1 - me.c]
            chunks.append((False, k, sender.start(src, twin_b.at[k], me.partner())))

    stage = []
    for is_a, k, copy in chunks:
        copy.wait_recv()
        x, to_x = me.along_x(k)
        y, to_y = me.along_y(k)

        def add_a(z, carry):
            for j in range(n_y):
                total = part[x // n_lo, j, z, x % n_lo, me.c] + twin_a[k, j, z]
                if k:
                    packed_a[k - 1, j, z] = total.astype(bf16)
                else:
                    twin_a[k, j, z] = total
            return carry

        def add_b(z, carry):
            for i in range(n_hi):
                for j in range(n_lo):
                    total = part[i, y, half + z, j, me.c] + twin_b[k, i, z, j]
                    if k:
                        packed_b[k - 1, i, j, z] = total.astype(bf16)
                    else:
                        twin_b[k, i, z, j] = total
            return carry

        lax.fori_loop(0, half, add_a if is_a else add_b, 0)
        if k and is_a:
            stage.append(sender.start(packed_a.at[k - 1], in_a.at[k - 1], to_x))
        elif k:
            stage.append(sender.start(packed_b.at[k - 1], in_b.at[k - 1], to_y))
    for copy in stage:
        copy.wait_recv()

    def add_plane(z, carry):
        for j in range(n_y):
            total = twin_a[0, j, z]
            for k in range(n_x - 1):
                total = total + in_a[k, j, z].astype(f32)
            twin_a[0, j, z] = total
        for i in range(n_hi):
            for j in range(n_lo):
                total = twin_b[0, i, z, j]
                for k in range(n_y - 1):
                    total = total + in_b[k, i, j, z].astype(f32)
                twin_b[0, i, z, j] = total
        return carry

    lax.fori_loop(0, half, add_plane, 0)

    stage = []
    for k in range(1, n_y):
        y, device = me.along_y(k)
        stage.append(sender.start(twin_a.at[0, y], in_a2.at[k - 1], device))
    for k in range(1, n_x):
        x, device = me.along_x(k)
        src = twin_b.at[0, x // n_lo, :, x % n_lo]
        stage.append(sender.start(src, in_b2.at[k - 1], device))
    for k in early:
        turn_cold(k)
    for copy in stage:
        copy.wait_recv()

    def add_line(z, carry):
        total = twin_a[0, me.y, z]
        for k in range(n_y - 1):
            total = total + in_a2[k, z]
        line[z] = total
        total = twin_b[0, me.x_hi, z, me.x_lo]
        for k in range(n_x - 1):
            total = total + in_b2[k, z]
        line[half + z] = total
        return carry

    lax.fori_loop(0, half, add_line, 0)

    stage = []
    for k in range(1, n_z):
        z, device = me.along_z(k)
        stage.append(sender.start(line.at[z], in_z.at[k - 1], device))
    for k in near_first[n_z // 2 :]:
        turn_cold(k)
    for copy in stage:
        copy.wait_recv()
    total = line[me.z]
    for k in range(n_z - 1):
        total = total + in_z[k]
    grad[...] = total
    fresh[...] = (old[...] - 0.1 * total).astype(bf16)

    lines = spread_lines(me, fresh, spread, plane_a, plane_b, sender, near)
    next(lines)

    for copy in kept:
        copy.wait()
    for copy in sent:
        copy.wait_recv()

    def xa(x):
        return cold_ya.at[:, :, x // n_lo, x % n_lo]

    def yb(y):
        return cold_xb.at[:, :, y]

    kept = [near.start(xa(me.x), cold_xa.at[me.x]), near.start(yb(me.y), cold_yb.at[:, me.y])]
    sent = []
    for k in range(1, n_x):
        x, device = me.along_x(k)
        sent.append(sender.start(xa(x), cold_xa.at[me.x], device))
    for k in range(1, n_y):
        y, device = me.along_y(k)
        sent.append(sender.start(yb(y), cold_yb.at[:, me.y], device))

    next(lines)
    next(lines)

    def swap_cold():
        for copy in kept:
            copy.wait()
        for copy in sent:
            copy.wait_recv()
        own, other = [], []
        for k in range(n_z):
            src = cold_xa if k < half else cold_yb
            dst = cold.at[me.c, :, :, (me.z + n_z - k) % n_z]
            own.append(near.start(src.at[:, :, k % half, me.c], dst))
            other.append(sender.start(src.at[:, :, k % half, 1 - me.c], dst, me.partner()))
        return own, other

    own, other = spread_planes(me, plane_a, plane_b, full, sender, near, swap_cold)
    for copy in own:
        copy.wait()
    for copy in other:
        copy.wait_recv()
    sender.finish()


def update_hot(counts, high, rest, old, slots, dims):
    n_hi, n_y, n_z, n_lo, _ = dims
    n_x, half = n_hi * n_lo, n_z // 2
    tile = old.shape
    f32, bf16 = jnp.float32, jnp.bfloat16
    unit = slots.shape[-2:]
    n_core = dims[4]
    grad, full, cold = pl.pallas_call(
        functools.partial(update_kernel, dims),
        out_shape=(
            jax.ShapeDtypeStruct(tile, f32),
            jax.ShapeDtypeStruct((*dims, *tile), bf16),
            jax.ShapeDtypeStruct((n_core, n_x, n_y, n_z, *unit), bf16),
        ),
        in_specs=[IN_VMEM] * 5,
        out_specs=(IN_VMEM,) * 3,
        scratch_shapes=[
            pltpu.VMEM((*dims, *tile), f32),
            pltpu.VMEM((n_z, n_hi, n_y, n_lo, n_core, *unit), bf16),
            pltpu.VMEM((n_y, half, n_hi, n_lo, n_core, *unit), bf16),
            pltpu.VMEM((n_x, n_y, half, n_core, *unit), bf16),
            pltpu.VMEM((n_x, half, n_y, n_core, *unit), bf16),
            pltpu.VMEM((n_x, n_y, half, n_core, *unit), bf16),
            pltpu.VMEM((n_x, n_y, half, *tile), f32),
            pltpu.VMEM((n_y, n_hi, half, n_lo, *tile), f32),
            pltpu.VMEM((n_x - 1, n_y, half, *tile), bf16),
            pltpu.VMEM((n_y - 1, n_hi, n_lo, half, *tile), bf16),
            pltpu.VMEM((n_x - 1, n_y, half, *tile), bf16),
            pltpu.VMEM((n_y - 1, n_hi, n_lo, half, *tile), bf16),
            pltpu.VMEM((n_y - 1, half, *tile), f32),
            pltpu.VMEM((n_x - 1, half, *tile), f32),
            pltpu.VMEM((n_z, *tile), f32),
            pltpu.VMEM((n_z - 1, *tile), f32),
            pltpu.VMEM(tile, bf16),
            pltpu.VMEM((n_z, *tile), bf16),
            pltpu.VMEM((n_y, half, *tile), bf16),
            pltpu.VMEM((n_hi, half, n_lo, *tile), bf16),
            *semaphores((half + 7) * (n_x + n_y) + 4 * n_z - 2 * half - 13, 2 * n_z + 8),
        ],
        compiler_params=pltpu.CompilerParams(collective_id=1, has_side_effects=True),
        name="update_hot",
    )(counts, high, rest, old, slots.reshape(*dims, *unit))
    return grad, full.reshape(-1, tile[1]), cold.reshape(-1, unit[1])


def body(dims, table, hot_slot, cold_row, cold_bag, hot_pick, dense, label):
    n = math.prod(dims)
    n_table, width = table.shape
    samples = dense.shape[0]
    cap = cold_row.shape[2]
    slots = cold_row.shape[1] * cap
    f32, bf16 = jnp.float32, jnp.bfloat16
    rounded = table.astype(bf16)

    asked, plane_a, plane_b, hot_old, counts = request_rows(
        cold_row[0], table, hot_slot, hot_pick, dims
    )
    arrived = asked.transpose(1, 3, 4, 2, 0, 5).reshape(slots)
    asked = asked.reshape(slots)

    row_ids = jnp.arange(n_table, dtype=jnp.int32)
    at_row = (arrived[:, None] == row_ids[None, :]).astype(bf16)
    looked = jnp.dot(at_row, rounded, preferred_element_type=f32).astype(bf16)
    returned = exchange(looked.reshape(n, cap, width)).reshape(slots, width)

    bags = cold_bag[0].reshape(slots)
    sample_ids = jnp.arange(samples, dtype=jnp.int32)
    selector = (sample_ids[:, None] == bags[None, :]).astype(bf16)
    hot_copy = finish_gather(plane_a, plane_b, dims)
    first = (((0,), (0,)), ((), ()))
    hot_pooled = lax.dot_general(counts, hot_copy, first, preferred_element_type=f32)
    pooled = jnp.dot(selector, returned, preferred_element_type=f32) + hot_pooled
    score = jnp.sum(pooled * dense, axis=1) / width**0.5
    err = jax.nn.sigmoid(score) - label.astype(f32)
    grad = err[:, None] * dense
    high, rest = split_bf16(grad)

    slot_grad = lax.dot_general(selector, high, first, preferred_element_type=f32).astype(bf16)
    own_grad, hot_new, delivered = update_hot(
        counts, high, rest, hot_old, slot_grad.reshape(n, cap, width), dims
    )

    from_row = (row_ids[:, None] == asked[None, :]).astype(bf16)
    table_grad = jnp.dot(from_row, delivered, preferred_element_type=f32)
    at_hot = (row_ids[:, None] == hot_slot[None, :]).astype(f32)
    table_grad = table_grad + jnp.dot(
        at_hot, own_grad, precision=lax.Precision.HIGHEST, preferred_element_type=f32
    )
    new_table = table - 0.1 * table_grad
    return (pooled, new_table, hot_new.astype(f32))


def solution(mesh, dims=SHAPE):
    placed = (
        P(AXES, None),
        P(AXES),
        P(AXES, None, None),
        P(AXES, None, None),
        P(AXES, None),
        P(AXES, None),
        P(AXES),
    )
    return jax.shard_map(
        functools.partial(body, dims),
        mesh=mesh,
        in_specs=placed,
        out_specs=(P(AXES, None), P(AXES, None), P()),
        check_vma=False,
    )
```
